32 devices in a mesh: sect: 4 (over y, x), tile: 8 (over z, core).
Axes of the slice: x: 2, y: 2, z: 4, core: 2. Of those that a mesh axis runs over, the one named last changes fastest.
Arguments:
- zonal: float32 [4, 64, 512], P('sect', 'tile'), may hold values from -1.5 to 1.5
- merid: float32 [4, 64, 512], P('sect', 'tile'), may hold values from -1.5 to 1.5
- height: float32 [4, 64, 512], P('sect', 'tile'), may hold values from -6 to 6
- level_kappa: float32 [4], replicated, may hold values from 0.2 to 2
- sea: int32 [64, 512], P('tile'), may hold values 0 or 1
- flags: int32 [4, 64, 512], P(None, 'tile', 'sect'), may hold values 0 or 1
- conc: float32 [12, 4, 64, 512], P(None, None, 'tile', 'sect'), may hold values from 0.1 to 2
- react: float32 [12, 12], replicated, may hold values from -1.2 to 1.2
- absorb: float32 [12], replicated, may hold values from 0.05 to 1
- light: float32 [4], replicated, may hold values from 0.1 to 1
Outputs:
- conc_out: float32 [12, 4, 64, 512], P(None, None, 'tile', 'sect')
- zonal_out: float32 [4, 64, 512], P('sect', 'tile')
- merid_out: float32 [4, 64, 512], P('sect', 'tile')
- height_out: float32 [4, 64, 512], P('sect', 'tile')
The draws below stay inside these ranges and needn't reach their ends.
All inputs are finite; a program needn't handle non-finite values. No bound on the sum of `sea` or of `flags` on one device may be relied on, other than what follows from the above.
Results may differ from the reference program's by a relative error of at most 0.00022.
Values sent between devices are 32-bit elements; how exact they have to be, the bound alone decides.
A program may use at most 64 MiB of HBM per device.

```python
import math
import jax
import jax.numpy as jnp
from jax import lax

NTR = 12
STEPS = 4
INTERVALS = 2
NZ = 4
NY = 64
NX = 512


def with_ends(entries, rng, least, high):
    dims = entries.shape
    place = [jax.random.randint(jax.random.fold_in(rng, axis), (), 0, dims[axis]) for axis in range(len(dims))]
    entries = entries.at[tuple(place)].set(least)
    longest = dims.index(max(dims))
    place[longest] = (place[longest] + 1) % dims[longest]
    return entries.at[tuple(place)].set(high)


def block_levels(rng, dims, split, smallest, largest):
    def one(axis_at, blocks):
        heights = jax.random.uniform(jax.random.fold_in(jax.random.fold_in(rng, 6), axis_at), (blocks,), jnp.float32, smallest / len(split), largest / len(split))
        return jnp.repeat(jnp.exp(heights), dims[axis_at] // blocks).reshape((-1,) + (1,) * (len(dims) - axis_at - 1))

    level = one(*split[0])
    for cut in split[1:]:
        level = level * one(*cut)
    return level


def gaussian(own_key, extent, deviation, bound, pieces=(), kind=jnp.bfloat16):
    values = deviation * jax.random.normal(own_key, extent, jnp.float32)
    if pieces:
        values = values * block_levels(own_key, extent, pieces, -0.22, 0.18)
    return jnp.clip(values, -bound, bound).astype(kind)


def setup_inputs(seed: int = 0) -> dict:
    key_list = jax.random.split(jax.random.key(seed), 11)
    return {
        "zonal": gaussian(key_list[0], (NZ, NY, NX), 0.3, 1.5, ((0, 4), (1, 8)), jnp.float32),
        "merid": gaussian(key_list[1], (NZ, NY, NX), 0.3, 1.5, ((0, 4), (1, 8)), jnp.float32),
        "height": gaussian(key_list[2], (NZ, NY, NX), 1.0, 6.0, ((0, 4), (1, 8)), jnp.float32),
        "level_kappa": jnp.clip(jnp.exp(jax.random.uniform(key_list[3], (NZ,), jnp.float32, math.log(0.2), math.log(2.0))), 0.2, 2.0),
        "sea": with_ends((jax.random.randint(key_list[4], (NY, NX), 0, 8) < 7).astype(jnp.int32), jax.random.fold_in(key_list[4], 1), 0, 1),
        "flags": with_ends((jax.random.randint(key_list[5], (NZ, NY, NX), 0, 2) < 1).astype(jnp.int32), jax.random.fold_in(key_list[5], 1), 0, 1),
        "conc": jnp.clip(jnp.exp(math.log(2.0) - 2.9957323 * jax.random.uniform(key_list[6], (NTR, NZ, NY, NX), jnp.float32) ** block_levels(key_list[6], (NTR, NZ, NY, NX), ((2, 8), (3, 4)), -0.2, 0.2)), 0.1, 2.0),
        "react": gaussian(key_list[7], (NTR, NTR), 0.3, 1.2, (), jnp.float32),
        "absorb": jnp.clip(jnp.exp(jax.random.uniform(key_list[8], (NTR,), jnp.float32, math.log(0.05), math.log(1.0))), 0.05, 1.0),
        "light": jnp.clip(jnp.exp(jax.random.uniform(key_list[9], (NZ,), jnp.float32, math.log(0.1), math.log(1.0))), 0.1, 1.0),
    }


time_step = 0.1
gravity = 1.0
coriolis = 0.3
viscosity = 0.05
heat_coupling = 0.05
tracer_step = 0.5
stir_gain = 4.0


def centred(field, axis):
    return 0.5 * (jnp.roll(field, -1, axis) - jnp.roll(field, 1, axis))


def laplace(field):
    total = jnp.roll(field, -1, 1) + jnp.roll(field, 1, 1)
    total = total + jnp.roll(field, -1, 2) + jnp.roll(field, 1, 2)
    return total - 4.0 * field


def upwind(conc, speed, flag, axis):
    ahead = jnp.roll(conc, -1, axis)
    behind = jnp.roll(conc, 1, axis)
    upper = jnp.maximum(speed, 0.0) * (conc - behind) + jnp.minimum(speed, 0.0) * (ahead - conc)
    middle = 0.5 * speed * (ahead - behind)
    return jnp.where(flag == 1, upper, middle)


def column_solve(starred, kappa):
    levels = starred.shape[1]
    couple = [tracer_step * 0.5 * (kappa[k] + kappa[k + 1]) for k in range(levels - 1)]
    factor = []
    partial_rhs = []
    for k in range(levels):
        lower = couple[k - 1] if k > 0 else jnp.zeros_like(kappa[0])
        upper = couple[k] if k < levels - 1 else jnp.zeros_like(kappa[0])
        diagonal = 1.0 + lower + upper
        if k == 0:
            denom = diagonal
            rhs_now = starred[:, 0] / denom
        else:
            denom = diagonal + lower * factor[k - 1]
            rhs_now = (starred[:, k] + lower * partial_rhs[k - 1]) / denom
        factor.append(-upper / denom)
        partial_rhs.append(rhs_now)
    result = [None] * levels
    result[levels - 1] = partial_rhs[levels - 1]
    for k in range(levels - 2, -1, -1):
        result[k] = partial_rhs[k] - factor[k] * result[k + 1]
    return jnp.stack(result, axis=1)


def reference(zonal, merid, height, level_kappa, sea, flags, conc, react, absorb, light):
    wet = sea.astype(jnp.float32)
    forcing = jnp.zeros(height.shape, jnp.float32)
    for interval in range(INTERVALS):
        zonal_sum = jnp.zeros(zonal.shape, jnp.float32)
        merid_sum = jnp.zeros(merid.shape, jnp.float32)
        for step in range(STEPS):
            height = height - time_step * (centred(zonal, 2) + centred(merid, 1)) + time_step * heat_coupling * forcing
            zonal_new = wet * (zonal + time_step * (coriolis * merid - gravity * centred(height, 2) + viscosity * laplace(zonal)))
            merid_new = wet * (merid + time_step * (-coriolis * zonal - gravity * centred(height, 1) + viscosity * laplace(merid)))
            zonal, merid = zonal_new, merid_new
            zonal_sum = zonal_sum + zonal
            merid_sum = merid_sum + merid
        zonal_mean = zonal_sum / STEPS
        merid_mean = merid_sum / STEPS
        kappa = level_kappa[:, None, None] * (1.0 + stir_gain * (zonal_mean * zonal_mean + merid_mean * merid_mean))
        moving = upwind(conc, zonal_mean, flags, 3) + upwind(conc, merid_mean, flags, 2)
        starred = conc - tracer_step * wet * moving
        mixed = column_solve(starred, kappa)
        growth = jnp.einsum("ij,jzyx->izyx", react, mixed, precision=lax.Precision.HIGHEST)
        conc = mixed + tracer_step * wet * growth
        if interval + 1 < INTERVALS:
            forcing = light[:, None, None] * jnp.einsum("k,kzyx->zyx", absorb, conc, precision=lax.Precision.HIGHEST)
    return conc, zonal, merid, height
```

```python
import functools

import jax
import jax.numpy as jnp
from jax import lax
from jax.experimental import pallas as pl
from jax.experimental.pallas import tpu as pltpu
from jax.sharding import PartitionSpec as P

STEPS = 4
INTERVALS = 2

time_step = 0.1
gravity = 1.0
coriolis = 0.3
viscosity = 0.05
heat_coupling = 0.05
tracer_step = 0.5
stir_gain = 4.0

LANES = 128
EDGE = 4 * STEPS
NEAR = EDGE // 2
FIRST = 4
SECOND = 2


def ocean_steps(zonal, merid, height, wet, forced, keep):
    tall, wide = zonal.shape

    def east(a):
        return pltpu.roll(a, wide - 1, 1)

    def west(a):
        return pltpu.roll(a, 1, 1)

    def north(a):
        return pltpu.roll(a, tall - 1, 0)

    def south(a):
        return pltpu.roll(a, 1, 0)

    keep_rate = time_step * viscosity
    self_rate = 1.0 / keep_rate - 4.0
    turn_rate = time_step * coriolis / keep_rate
    steep = 0.5 * gravity * time_step / keep_rate
    gain = keep_rate * wet
    rise = steep * height
    if forced is not None:
        forced = steep * forced
    zonal_sum = merid_sum = None
    for step in range(STEPS):
        ze, zw, zn, zs = east(zonal), west(zonal), north(zonal), south(zonal)
        me, mw, mn, ms = east(merid), west(merid), north(merid), south(merid)
        rise = rise - (0.5 * time_step * steep) * ((ze - zw) + (mn - ms))
        zonal_part = ((ze + zw) + (zn + zs)) + (self_rate * zonal + turn_rate * merid)
        merid_part = ((me + mw) + (mn + ms)) + (self_rate * merid - turn_rate * zonal)
        if forced is not None:
            rise = rise + forced
        zonal_new = gain * (zonal_part - (east(rise) - west(rise)))
        merid_new = gain * (merid_part - (north(rise) - south(rise)))
        zonal, merid = zonal_new, merid_new
        zonal_sum = zonal[keep] if step == 0 else zonal_sum + zonal[keep]
        merid_sum = merid[keep] if step == 0 else merid_sum + merid[keep]
    return zonal[keep], merid[keep], (1.0 / steep) * rise[keep], zonal_sum / STEPS, merid_sum / STEPS


def column_terms(speeds, upwind, half_wet, kappa_in):
    levels = len(speeds)
    kappa, stencil = [], []
    for k in range(levels):
        along_x, along_y = speeds[k]
        kappa.append(kappa_in[k] * (1.0 + stir_gain * (along_x * along_x + along_y * along_y)))
        terms = []
        for speed in (along_x, along_y):
            terms.append(half_wet * jnp.where(upwind[k], jnp.maximum(speed, 0.0), 0.5 * speed))
            terms.append(half_wet * jnp.where(upwind[k], jnp.minimum(speed, 0.0), 0.5 * speed))
        stencil.append(terms)
    couple = [tracer_step * 0.5 * (kappa[k] + kappa[k + 1]) for k in range(levels - 1)]
    out, factor = [], None
    for k in range(levels):
        denom = 1.0
        if k > 0:
            denom = denom + couple[k - 1]
        if k < levels - 1:
            denom = denom + couple[k]
        if k > 0:
            denom = denom + couple[k - 1] * factor
        inverse = 1.0 / denom
        px, qx, py, qy = stencil[k]
        out.append(
            dict(
                centre=inverse * (1.0 - ((px - qx) + (py - qy))),
                west=inverse * px,
                east=inverse * qx,
                south=inverse * py,
                north=inverse * qy,
                lower=inverse * couple[k - 1] if k > 0 else None,
                upper=inverse * couple[k] if k < levels - 1 else None,
            )
        )
        factor = -out[k]["upper"] if k < levels - 1 else None
    return out


def solve_column(terms, cells):
    levels = len(terms)
    partial = []
    for k in range(levels):
        t = terms[k]
        base, west, east, south, north = cells(k)
        now = t["centre"] * base + (t["west"] * west - t["east"] * east) + (t["south"] * south - t["north"] * north)
        if k > 0:
            now = now + t["lower"] * partial[k - 1]
        partial.append(now)
    for k in range(levels - 2, -1, -1):
        partial[k] = partial[k] + terms[k]["upper"] * partial[k + 1]
    return partial


def kernel(
    sects,
    tiles,
    zonal_in,
    merid_in,
    height_in,
    sea_in,
    flags_in,
    conc_in,
    kappa_hbm,
    react_hbm,
    absorb_hbm,
    light_hbm,
    conc_out,
    zonal_out,
    merid_out,
    height_out,
    kappa_in,
    react_in,
    absorb_in,
    light_in,
    own,
    sea,
    flags,
    conc,
    react_d,
    base,
    west_v,
    east_v,
    south_v,
    north_v,
    cols_send,
    cols_recv,
    rows_send,
    rows_recv,
    blk_send,
    blk_recv,
    sea_send,
    sea_recv,
    mix_send,
    mix_recv,
    rest_send,
    rest_recv,
    strip_send,
    strip_recv,
    wet_all,
    state,
    state_edge,
    means,
    last_means,
    force,
    out_send,
    out_recv,
    local_sem,
    blk_ssem,
    blk_rsem,
    sea_ssem,
    sea_rsem,
    mix_ssem,
    mix_rsem,
    state_ssem,
    state_rsem,
    force_ssem,
    force_rsem,
    strip_ssem,
    strip_rsem,
    halo_ssem,
    halo_rsem,
    out_ssem,
    out_rsem,
    known_sem,
):
    me_s = lax.axis_index("sect")
    me_t = lax.axis_index("tile")
    tracers, levels, rows, columns = conc_in.shape
    depth = zonal_in.shape[0]
    bands = 3
    far = bands

    def sect_at(offset):
        return lax.rem(me_s + (offset + sects), sects)

    def tile_at(offset):
        return lax.rem(me_t + (offset + tiles), tiles)

    def hops(s, t):
        count = t // 2
        for bit in range((sects - 1).bit_length()):
            count = count + lax.rem(s // (1 << bit), 2)
        return count

    def place(s, t):
        return ((2 * hops(s, t) + 1 - lax.rem(t, 2)) * tiles + t) * sects + s

    def across(m):
        s = me_s
        for bit in range((sects - 1).bit_length()):
            if m >> bit & 1:
                s = s + (1 << bit) - 2 * (1 << bit) * lax.rem(me_s // (1 << bit), 2)
        return s

    near = sorted(range(sects), key=lambda m: (m.bit_count(), m))
    peers = [(m, across(m), dt, tile_at(dt)) for dt in (1, 0, -1) for m in near if m or dt]
    mine = place(me_s, me_t)
    later, sooner, greet = [], [], []
    for m, s, dt, t in peers:
        is_later = place(s, t) > mine
        if m and dt:
            wraps = (me_t + dt < 0) | (me_t + dt >= tiles)
            ahead = hops(s, t) - hops(me_s, me_t)
            mutual = wraps & (ahead <= 1) & (ahead >= -1)
            later.append(is_later & jnp.logical_not(mutual))
            sooner.append(jnp.logical_not(is_later) & jnp.logical_not(mutual))
            greet.append(is_later | mutual)
        else:
            later.append(is_later)
            sooner.append(jnp.logical_not(is_later))
            greet.append(is_later)

    def remote(src, dst, send, recv, to_s, to_t):
        return pltpu.make_async_remote_copy(
            src_ref=src,
            dst_ref=dst,
            send_sem=send,
            recv_sem=recv,
            device_id=(to_s, to_t),
            device_id_type=pl.DeviceIdType.MESH,
        )

    fields_in = (zonal_in, merid_in, height_in)
    ocean_local = [pltpu.make_async_copy(field, own.at[f], local_sem.at[f]) for f, field in enumerate(fields_in)]
    ocean_local.append(pltpu.make_async_copy(sea_in, sea, local_sem.at[3]))
    tracer_local = [
        pltpu.make_async_copy(src, dst, local_sem.at[4 + i])
        for i, (src, dst) in enumerate(
            (
                (conc_in, conc),
                (flags_in, flags),
                (react_hbm, react_in),
                (absorb_hbm, absorb_in),
                (kappa_hbm, kappa_in),
                (light_hbm, light_in),
            )
        )
    ]
    barrier = pltpu.get_barrier_semaphore()
    @pl.when(me_t == 0)
    def _():
        for s in [across(m) for m in near[::-1]]:
            pl.semaphore_signal(barrier, inc=1, device_id=(s, tiles - 2), device_id_type=pl.DeviceIdType.MESH)

    heard = 0
    for n, (_, s, _, t) in reversed(list(enumerate(peers))):
        heard = heard + jnp.where(later[n], 0, 1)

        @pl.when(greet[n])
        def _():
            pl.semaphore_signal(barrier, inc=1, device_id=(s, t), device_id_type=pl.DeviceIdType.MESH)

    for copy in ocean_local + tracer_local:
        copy.start()
    heard = heard + jnp.where(me_t == tiles - 2, sects, 0)

    @pl.when(heard > 0)
    def _():
        pl.semaphore_wait(barrier, heard)

    for n, (_, s, dt, t) in enumerate(peers):

        @pl.when(sooner[n])
        def _():
            pl.semaphore_signal(
                known_sem.at[1 - dt, me_s], inc=1, device_id=(s, t), device_id_type=pl.DeviceIdType.MESH
            )

    lane = lax.broadcasted_iota(jnp.int32, (rows, columns), 1)
    row = lax.broadcasted_iota(jnp.int32, (rows, columns), 0)
    low_half = lane < LANES // 2

    for copy in ocean_local:
        copy.wait()

    def lanes_of(s):
        return slice((s % sects) * columns, (s % sects + 1) * columns)

    sea_f = [sea[:, lanes_of(s)].astype(jnp.float32) for s in range(sects)]
    for d in range(sects):
        for ld in range(depth):
            packed = None
            for f in range(4):
                if f < 3:
                    blk_send[d, 4 * ld + f] = own[f, ld, :, lanes_of(d)]
                    after, before = own[f, ld, :, lanes_of(d + 1)], own[f, ld, :, lanes_of(d - 1)]
                else:
                    after, before = sea_f[(d + 1) % sects], sea_f[(d - 1) % sects]
                edge = jnp.where(low_half, after, before)
                if f == 0:
                    packed = edge
                else:
                    inside = (lane >= 2 * EDGE * f - EDGE) & (lane < 2 * EDGE * f + EDGE)
                    packed = jnp.where(inside, pltpu.roll(edge, 2 * EDGE * f, 1), packed)
            blk_send[d, 4 * ld + 3] = packed
    own_columns = pl.ds(pl.multiple_of(me_s * columns, LANES), columns)
    wet_cols = sea[:, own_columns].astype(jnp.float32)
    is_wet = wet_cols == 1.0
    sea_send[...] = wet_cols

    def blk_copy(j, s_slot, send, to_s, to_t, src):
        return remote(blk_send.at[src], blk_recv.at[j, s_slot], send, blk_rsem.at[j, s_slot], to_s, to_t)

    sent = []
    to_peer = [
        blk_copy(1 - dt, me_s, blk_ssem.at[1 + dt, s], s, t, s) for _, s, dt, t in peers
    ]
    seas = [
        remote(sea_send, sea_recv.at[1 - dt], sea_ssem.at[1 + dt], sea_rsem.at[1 - dt], me_s, tile_at(dt))
        for dt in (1, -1)
    ]
    over = [blk_copy(far, me_s, blk_ssem.at[far, across(m)], across(m), 0, across(m)) for m in near[::-1]]
    over.append(remote(sea_send, sea_recv.at[far], sea_ssem.at[far], sea_rsem.at[far], me_s, 0))

    @pl.when(me_t == tiles - 2)
    def _():
        for copy in over[sects:] + over[:sects]:
            copy.start()

    def begin(n):
        m, _, dt, _ = peers[n]
        if not m:
            seas[0 if dt == 1 else 1].start()
        to_peer[n].start()

    for n in sorted(range(len(peers)), key=lambda n: (-peers[n][2] % bands, -n)):

        @pl.when(jnp.logical_not(later[n]))
        def _():
            begin(n)

    blk_recv[1, me_s] = blk_send[me_s]
    sea_recv[1] = sea_send[...]
    for copy in tracer_local:
        copy.wait()

    cells = tracers * levels

    def react_and_pack(turn, heated):
        names = tracers + (1 if heated else 0)
        to_east = [jnp.zeros((rows, columns), jnp.float32) for _ in range(pl.cdiv(cells, LANES))]
        to_west = list(to_east)
        for k in range(levels):
            old = [conc[i, k] for i in range(tracers)]
            heat_d = None
            for i in range(names):
                n = i * levels + k
                if i < tracers:
                    growth = react_in[i, 0] * old[0]
                    for j in range(1, tracers):
                        growth = growth + react_in[i, j] * old[j]
                    new = old[i] + tracer_step * growth
                    kept = jnp.where(is_wet, new, old[i])
                    if heated:
                        a = absorb_in[i]
                        heat_d = a * new if i == 0 else heat_d + a * new
                        heat_b = a * kept if i == 0 else heat_b + a * kept
                else:
                    mix_send[k] = heat_d
                    rest_send[k] = heat_b
                    continue
                react_d[n] = new
                base[n] = kept
                rows_send[turn, 0, pl.ds(n, 1)] = new[rows - 1 : rows]
                rows_send[turn, 1, pl.ds(n, 1)] = new[0:1]
                p, at = divmod(n, LANES)
                here = lane == at
                turned = pltpu.roll(new, (at + 1) % columns, 1)
                to_east[p] = jnp.where(here, turned, to_east[p])
                turned = pltpu.roll(new, at, 1) if at else new
                to_west[p] = jnp.where(here, turned, to_west[p])
        for p in range(len(to_east)):
            cols_send[turn, 0, p] = to_east[p]
            cols_send[turn, 1, p] = to_west[p]
        copies = []
        for i, d in enumerate((1, -1)):
            copies.append(
                remote(
                    rows_send.at[turn, i],
                    rows_recv.at[turn, i],
                    halo_ssem.at[turn, i],
                    halo_rsem.at[turn, i],
                    me_s,
                    tile_at(d),
                )
            )
            copies.append(
                remote(
                    cols_send.at[turn, i],
                    cols_recv.at[turn, i],
                    halo_ssem.at[turn, 2 + i],
                    halo_rsem.at[turn, 2 + i],
                    sect_at(d),
                    me_t,
                )
            )
        return copies

    def shift_cells(turn):
        from_west = [cols_recv[turn, 0, p] for p in range(pl.cdiv(cells, LANES))]
        from_east = [cols_recv[turn, 1, p] for p in range(pl.cdiv(cells, LANES))]
        for n in range(cells):
            p, at = divmod(n, LANES)
            new = react_d[n]
            edge = pltpu.roll(from_west[p], columns - at, 1) if at else from_west[p]
            west_v[n] = jnp.where(lane == 0, edge, pltpu.roll(new, 1, 1))
            edge = pltpu.roll(from_east[p], columns - 1 - at, 1) if at < columns - 1 else from_east[p]
            east_v[n] = jnp.where(lane == columns - 1, edge, pltpu.roll(new, columns - 1, 1))
            edge = jnp.broadcast_to(rows_recv[turn, 0, pl.ds(n, 1)], (rows, columns))
            south_v[n] = jnp.where(row == 0, edge, pltpu.roll(new, 1, 0))
            edge = jnp.broadcast_to(rows_recv[turn, 1, pl.ds(n, 1)], (rows, columns))
            north_v[n] = jnp.where(row == rows - 1, edge, pltpu.roll(new, rows - 1, 0))

    def tracer_cells(i):
        def read(k):
            n = i * levels + k
            return base[n], west_v[n], east_v[n], south_v[n], north_v[n]

        return read

    halo0 = react_and_pack(0, True)
    for k in range(levels):
        rest_send[levels + k] = flags[k].astype(jnp.float32)
    per = LANES // NEAR
    for p in range(pl.cdiv(3 * levels, per)):
        to_east = to_west = jnp.zeros((rows, columns), jnp.float32)
        for at in range(min(per, 3 * levels - p * per)):
            q = p * per + at
            value = mix_send[q] if q < levels else rest_send[q - levels]
            here = (lane >= NEAR * at) & (lane < NEAR * at + NEAR)
            turned = pltpu.roll(value, (NEAR * at + NEAR) % LANES, 1)
            to_east = jnp.where(here, turned, to_east)
            turned = pltpu.roll(value, NEAR * at, 1) if at else value
            to_west = jnp.where(here, turned, to_west)
        strip_send[0, p] = to_east
        strip_send[1, p] = to_west
    sent.extend(seas)
    mixes, strips = [], []
    for i, dt in enumerate((1, -1)):
        mixes.append(remote(mix_send, mix_recv.at[i], mix_ssem.at[i], mix_rsem.at[i], me_s, tile_at(dt)))
    for i, ds in enumerate((1, -1)):
        for dt in (1, -1, 0):
            strips.append(
                remote(
                    strip_send.at[i],
                    strip_recv.at[i, 1 - dt],
                    strip_ssem.at[i, 1 - dt],
                    strip_rsem.at[i, 1 - dt],
                    sect_at(ds),
                    tile_at(dt),
                )
            )
    sent.extend(mixes + strips + halo0)
    for now in (1, 0, -1):
        for n, (_, s, dt, _) in enumerate(peers):
            if dt == now:

                @pl.when(later[n])
                def _():
                    pl.semaphore_wait(known_sem.at[1 + dt, s], 1)
                    begin(n)

        if now == 1:
            continue
        directions = (1, 0) if now == 0 else (-1,)
        for dt in directions:
            if dt:
                mixes[0 if dt == 1 else 1].start()
                halo0[0 if dt == 1 else 2].start()
            else:
                halo0[1].start()
                halo0[3].start()
            for i in range(2):
                strips[3 * i + (1, -1, 0).index(dt)].start()

    rest = remote(rest_send, rest_recv, mix_ssem.at[2], mix_rsem.at[2], me_s, 0)

    @pl.when(me_t == tiles - 1)
    def _():
        rest.start()


    for copy in seas:
        copy.wait_recv()

    def blk_wait(j, s):
        blk_copy(j, s, blk_ssem.at[0, 0], me_s, me_t, me_s).wait_recv()

    for j in (0, 2):
        blk_wait(j, me_s)
    in_edge = (lane < EDGE) | (lane >= LANES - EDGE)

    def wet_band(j):
        turned = pltpu.roll(blk_recv[j, me_s, 3], LANES - 6 * EDGE, 1)
        return jnp.concatenate([sea_recv[j], jnp.where(in_edge, turned, 0.0)], axis=1)

    for j in range(bands):
        wet_all[j * rows : (j + 1) * rows] = wet_band(j)
    centre = slice(rows, 2 * rows)

    def first_levels(group, slots, wet, target):
        for l in [group * FIRST * depth + ld for ld in range(FIRST * depth)]:
            s, ld = l // depth, lax.rem(l, depth)
            full = []
            packed = [blk_recv[j, s, 4 * ld + 3] for j in slots]
            for f in range(3):
                parts = []
                for j, pack in zip(slots, packed):
                    turned = pltpu.roll(pack, LANES - 2 * EDGE * f, 1) if f else pack
                    parts.append(jnp.concatenate([blk_recv[j, s, 4 * ld + f], turned], axis=1))
                full.append(jnp.concatenate(parts, axis=0))
            z, m, h, zm, mm = ocean_steps(*full, wet, None, (centre, slice(None)))
            for f, value in enumerate((z, m, h)):
                state[target, 3 * l + f] = value[:, 0:columns]
                state_edge[target, 3 * l + f] = value[:, columns:]
            for i, value in enumerate((zm, mm)):
                means[target, l, i] = value

    def first_interval(group, carry):
        for s in [group * FIRST + at for at in range(FIRST)]:

            @pl.when(s != me_s)
            def _():
                for j in range(bands):
                    blk_wait(j, s)

        first_levels(group, (0, 1, 2), wet_all[...], 1)
        return carry

    def beyond_interval(group, carry):
        for at in range(FIRST):
            blk_wait(far, group * FIRST + at)
        first_levels(group, (far, 0, 1), jnp.concatenate([wet_band(far), wet_all[0 : 2 * rows]], axis=0), 0)
        return carry

    lax.fori_loop(0, sects // FIRST, first_interval, 0)

    pair = LANES // (2 * NEAR)

    def pack_edges(buffer, slot, values):
        start = buffer.shape[1] - pl.cdiv(len(values), pair)
        for p in range(pl.cdiv(len(values), pair)):
            tile = values[p * pair]
            for i, value in enumerate(values[p * pair + 1 : (p + 1) * pair], 1):
                here = (lane >= 2 * NEAR * i - NEAR) & (lane < 2 * NEAR * i + NEAR)
                tile = jnp.where(here, pltpu.roll(value, 2 * NEAR * i, 1), tile)
            buffer[slot, start + p] = tile

    def with_edges(buffer, slot, q, count):
        start = buffer.shape[1] - pl.cdiv(count, pair)
        p, at = divmod(q, pair)
        edge = buffer[slot, start + p]
        if at:
            edge = pltpu.roll(edge, LANES - 2 * NEAR * at, 1)
        return jnp.concatenate([buffer[slot, q], edge], axis=1)

    pack_edges(state, 1, [state_edge[1, q] for q in range(3 * levels)])

    def neighbours(buffer, send, recv):
        return [
            remote(buffer.at[1], buffer.at[0], send.at[0], recv.at[0], me_s, tile_at(1)),
            remote(buffer.at[1], buffer.at[2], send.at[1], recv.at[1], me_s, tile_at(-1)),
        ]

    states = neighbours(state, state_ssem, state_rsem)
    forces = neighbours(force, force_ssem, force_rsem)

    def hand_on(copies):
        copies[1].start()

        @pl.when(me_t != tiles - 1)
        def _():
            copies[0].start()

    hand_on(states)
    for copy in mixes + strips:
        copy.wait_recv()

    def wide_tile(q, j):
        p, at = divmod(q, per)
        if j == 1:
            inner = mix_send[q] if q < levels else rest_send[q - levels]
        elif q < levels:
            inner = mix_recv[j // 2, q]
        else:
            inner = rest_recv[q - levels]
        west_part = pltpu.roll(strip_recv[0, j, p], LANES - NEAR - NEAR * at, 1)
        east_part = strip_recv[1, j, p]
        if at:
            east_part = pltpu.roll(east_part, LANES - NEAR * at, 1)
        return jnp.concatenate([inner, jnp.where(low_half, east_part, west_part)], axis=1)

    wide = columns + LANES

    def heat_band(j):
        speeds = [(means[j, k, 0], means[j, k, 1]) for k in range(levels)]
        upwind = [wide_tile(2 * levels + k, j) > 0.5 for k in range(levels)]
        terms = column_terms(speeds, upwind, tracer_step * wet_all[j * rows : (j + 1) * rows], kappa_in)
        band = slice(j * rows, (j + 1) * rows)

        def heat_cells(k):
            each = [wide_tile(k, i) for i in range(bands)]
            d = jnp.concatenate(each, axis=0)
            return (
                wide_tile(levels + k, j),
                pltpu.roll(each[j], 1, 1),
                pltpu.roll(each[j], wide - 1, 1),
                pltpu.roll(d, 1, 0)[band],
                pltpu.roll(d, bands * rows - 1, 0)[band],
            )

        edges = []
        for k, value in enumerate(solve_column(terms, heat_cells)):
            value = (time_step * heat_coupling) * (light_in[k] * value)
            force[j, k] = value[:, 0:columns]
            edges.append(value[:, columns:])
        pack_edges(force, j, edges)

    heat_band(1)
    hand_on(forces)

    half_wet = tracer_step * wet_cols
    upwind = [flags[k] == 1 for k in range(levels)]
    speeds = [tuple(means[1, k, i, :, 0:columns] for i in range(2)) for k in range(levels)]
    terms = column_terms(speeds, upwind, half_wet, kappa_in)
    for copy in halo0:
        copy.wait_recv()
    shift_cells(0)
    for i in range(tracers):
        for k, value in enumerate(solve_column(terms, tracer_cells(i))):
            conc[i, k] = value
    halo1 = react_and_pack(1, False)
    for copy in halo1:
        copy.start()
    sent.extend(halo1)

    @pl.when(me_t == 0)
    def _():
        over[sects].wait_recv()
        lax.fori_loop(0, sects // FIRST, beyond_interval, 0)
        pack_edges(state, 0, [state_edge[0, q] for q in range(3 * levels)])
        rest.wait_recv()
        heat_band(0)

    states[1].wait_recv()
    forces[1].wait_recv()

    @pl.when(me_t != 0)
    def _():
        states[0].wait_recv()
        forces[0].wait_recv()

    def out_copy(l):
        owner, ld = l // depth, l % depth
        return remote(
            out_send.at[l], out_recv.at[me_s, ld], out_ssem.at[l], out_rsem.at[me_s, ld], owner, me_t
        )

    def second_interval(group):
        for l in [group * SECOND + at for at in range(SECOND)]:
            whole = [
                jnp.concatenate([with_edges(state, j, 3 * l + f, 3 * levels) for j in range(bands)], axis=0)
                for f in range(3)
            ]
            forced = jnp.concatenate([with_edges(force, j, l, levels) for j in range(bands)], axis=0)
            z, m, h, zm, mm = ocean_steps(*whole, wet_all[...], forced, (centre, slice(0, columns)))
            last_means[l, 0] = zm
            last_means[l, 1] = mm
            for f, value in enumerate((z, m, h)):
                out_send[l, f] = value
        for l in [group * SECOND + at for at in range(SECOND)]:

            @pl.when(l // depth != me_s)
            def _():
                out_copy(l).start()

    for group in range(levels // SECOND):
        second_interval(group)
    for ld in range(depth):
        out_recv[me_s, ld] = out_send[me_s * depth + ld]

    upwind = [flags[k] == 1 for k in range(levels)]
    speeds = [(last_means[k, 0], last_means[k, 1]) for k in range(levels)]
    terms = column_terms(speeds, upwind, half_wet, kappa_in)
    for copy in halo1:
        copy.wait_recv()
    shift_cells(1)
    for i in range(tracers):
        for k, value in enumerate(solve_column(terms, tracer_cells(i))):
            conc_out[i, k] = value

    def gather(s, carry):
        @pl.when(s != me_s)
        def _():
            for ld in range(depth):
                remote(
                    out_send.at[0], out_recv.at[s, ld], out_ssem.at[0], out_rsem.at[s, ld], me_s, me_t
                ).wait_recv()

        return carry

    lax.fori_loop(0, sects, gather, 0)
    for s in range(sects):
        for ld in range(depth):
            for f, ref in enumerate((zonal_out, merid_out, height_out)):
                ref[ld, :, lanes_of(s)] = out_recv[s, ld, f]
    for copy in sent + [states[1], forces[1]]:
        copy.wait_send()

    for copy in to_peer:
        copy.wait_send()

    @pl.when(me_t != tiles - 1)
    def _():
        states[0].wait_send()
        forces[0].wait_send()

    @pl.when(me_t == tiles - 1)
    def _():
        rest.wait_send()

    @pl.when(me_t == tiles - 2)
    def _():
        for copy in over:
            copy.wait_send()


    def drain(l, carry):
        @pl.when(l // depth != me_s)
        def _():
            out_copy(l).wait_send()

        return carry

    lax.fori_loop(0, levels, drain, 0)


def put_out(*refs):
    copies = [
        pltpu.make_async_copy(src, dst, refs[8].at[i])
        for i, (src, dst) in enumerate(zip(refs[:4], refs[4:8]))
    ]
    for copy in copies:
        copy.start()
    for copy in copies:
        copy.wait()


def body(sects, tiles, zonal, merid, height, level_kappa, sea, flags, conc, react, absorb, light):
    tracers, levels, rows, columns = conc.shape
    depth, _, wide = zonal.shape
    assert rows >= NEAR and columns == LANES and INTERVALS == 2
    assert tiles > 3 and sects > 1 and levels == sects * depth and wide == sects * columns
    cells = tracers * levels
    packs = pl.cdiv(cells, LANES)
    padded = pl.cdiv(cells, 8) * 8
    strips = pl.cdiv(3 * levels, LANES // NEAR)
    pair = LANES // (2 * NEAR)
    f32 = jnp.float32
    dma = pltpu.SemaphoreType.DMA
    any_space = pl.BlockSpec(memory_space=pl.ANY)
    vmem = pl.BlockSpec(memory_space=pltpu.VMEM)
    results = pl.pallas_call(
        functools.partial(kernel, sects, tiles),
        out_shape=[
            pltpu.VMEM(conc.shape, f32),
            pltpu.VMEM(zonal.shape, f32),
            pltpu.VMEM(merid.shape, f32),
            pltpu.VMEM(height.shape, f32),
        ],
        in_specs=[pl.BlockSpec(memory_space=pltpu.HBM)] * 10,
        out_specs=[vmem] * 4,
        scratch_shapes=[
            pltpu.SMEM(level_kappa.shape, f32),
            pltpu.SMEM(react.shape, f32),
            pltpu.SMEM(absorb.shape, f32),
            pltpu.SMEM(light.shape, f32),
            pltpu.VMEM((3, depth, rows, wide), f32),
            pltpu.VMEM((rows, wide), jnp.int32),
            pltpu.VMEM(flags.shape, jnp.int32),
            pltpu.VMEM(conc.shape, f32),
        ]
        + [pltpu.VMEM((cells, rows, columns), f32)] * 6
        + [
            pltpu.VMEM((2, 2, packs, rows, columns), f32),
            pltpu.VMEM((2, 2, packs, rows, columns), f32),
            pltpu.VMEM((2, 2, padded, columns), f32),
            pltpu.VMEM((2, 2, padded, columns), f32),
            pltpu.VMEM((sects, 4 * depth, rows, columns), f32),
            pltpu.VMEM((4, sects, 4 * depth, rows, columns), f32),
            pltpu.VMEM((rows, columns), f32),
            pltpu.VMEM((4, rows, columns), f32),
            pltpu.VMEM((levels, rows, columns), f32),
            pltpu.VMEM((2, levels, rows, columns), f32),
            pltpu.VMEM((2 * levels, rows, columns), f32),
            pltpu.VMEM((2 * levels, rows, columns), f32),
            pltpu.VMEM((2, strips, rows, columns), f32),
            pltpu.VMEM((2, 3, strips, rows, columns), f32),
            pltpu.VMEM((3 * rows, columns + LANES), f32),
            pltpu.VMEM((3, 3 * levels + pl.cdiv(3 * levels, pair), rows, columns), f32),
            pltpu.VMEM((2, 3 * levels, rows, columns), f32),
            pltpu.VMEM((2, levels, 2, rows, columns + LANES), f32),
            pltpu.VMEM((levels, 2, rows, columns), f32),
            pltpu.VMEM((3, levels + pl.cdiv(levels, pair), rows, columns), f32),
            pltpu.VMEM((levels, 3, rows, columns), f32),
            pltpu.VMEM((sects, depth, 3, rows, columns), f32),
            dma((10,)),
            dma((4, sects)),
            dma((4, sects)),
            dma((4,)),
            dma((4,)),
            dma((3,)),
            dma((3,)),
            dma((2,)),
            dma((2,)),
            dma((2,)),
            dma((2,)),
            dma((2, 3)),
            dma((2, 3)),
            dma((2, 4)),
            dma((2, 4)),
            dma((levels,)),
            dma((sects, depth)),
            pltpu.SemaphoreType.REGULAR((3, sects)),
        ],
        compiler_params=pltpu.CompilerParams(collective_id=0, has_side_effects=True),
        name="coupled",
    )(zonal, merid, height, sea, flags, conc, level_kappa, react, absorb, light)
    return pl.pallas_call(
        put_out,
        out_shape=[jax.ShapeDtypeStruct(r.shape, f32) for r in results],
        in_specs=[vmem] * 4,
        out_specs=[any_space] * 4,
        scratch_shapes=[dma((4,))],
        name="put_out",
    )(*[pltpu.with_memory_space_constraint(r, pltpu.VMEM) for r in results])


def solution(mesh):
    placed = (
        P("sect", "tile", None),
        P("sect", "tile", None),
        P("sect", "tile", None),
        P(),
        P("tile", None),
        P(None, "tile", "sect"),
        P(None, None, "tile", "sect"),
        P(),
        P(),
        P(),
    )
    return jax.shard_map(
        functools.partial(body, mesh.shape["sect"], mesh.shape["tile"]),
        mesh=mesh,
        in_specs=placed,
        out_specs=(
            P(None, None, "tile", "sect"),
            P("sect", "tile", None),
            P("sect", "tile", None),
            P("sect", "tile", None),
        ),
        check_vma=False,
    )
```

```python
import functools

import jax
import jax.numpy as jnp
from jax import lax
from jax.experimental import pallas as pl
from jax.experimental.pallas import tpu as pltpu
from jax.sharding import PartitionSpec as P

STEPS = 4
INTERVALS = 2

time_step = 0.1
gravity = 1.0
coriolis = 0.3
viscosity = 0.05
heat_coupling = 0.05
tracer_step = 0.5
stir_gain = 4.0

LANES = 128
EDGE = 4 * STEPS
NEAR = EDGE // 2
FIRST = 4
SECOND = 2


def ocean_steps(zonal, merid, height, wet, forced, keep):
    tall, wide = zonal.shape

    def east(a):
        return pltpu.roll(a, wide - 1, 1)

    def west(a):
        return pltpu.roll(a, 1, 1)

    def north(a):
        return pltpu.roll(a, tall - 1, 0)

    def south(a):
        return pltpu.roll(a, 1, 0)

    keep_rate = time_step * viscosity
    self_rate = 1.0 / keep_rate - 4.0
    turn_rate = time_step * coriolis / keep_rate
    steep = 0.5 * gravity * time_step / keep_rate
    gain = keep_rate * wet
    rise = steep * height
    if forced is not None:
        forced = steep * forced
    zonal_sum = merid_sum = None
    for step in range(STEPS):
        ze, zw, zn, zs = east(zonal), west(zonal), north(zonal), south(zonal)
        me, mw, mn, ms = east(merid), west(merid), north(merid), south(merid)
        rise = rise - (0.5 * time_step * steep) * ((ze - zw) + (mn - ms))
        zonal_part = ((ze + zw) + (zn + zs)) + (self_rate * zonal + turn_rate * merid)
        merid_part = ((me + mw) + (mn + ms)) + (self_rate * merid - turn_rate * zonal)
        if forced is not None:
            rise = rise + forced
        zonal_new = gain * (zonal_part - (east(rise) - west(rise)))
        merid_new = gain * (merid_part - (north(rise) - south(rise)))
        zonal, merid = zonal_new, merid_new
        zonal_sum = zonal[keep] if step == 0 else zonal_sum + zonal[keep]
        merid_sum = merid[keep] if step == 0 else merid_sum + merid[keep]
    return zonal[keep], merid[keep], (1.0 / steep) * rise[keep], zonal_sum / STEPS, merid_sum / STEPS


def column_terms(speeds, upwind, half_wet, kappa_in):
    levels = len(speeds)
    kappa, stencil = [], []
    for k in range(levels):
        along_x, along_y = speeds[k]
        kappa.append(kappa_in[k] * (1.0 + stir_gain * (along_x * along_x + along_y * along_y)))
        terms = []
        for speed in (along_x, along_y):
            terms.append(half_wet * jnp.where(upwind[k], jnp.maximum(speed, 0.0), 0.5 * speed))
            terms.append(half_wet * jnp.where(upwind[k], jnp.minimum(speed, 0.0), 0.5 * speed))
        stencil.append(terms)
    couple = [tracer_step * 0.5 * (kappa[k] + kappa[k + 1]) for k in range(levels - 1)]
    out, factor = [], None
    for k in range(levels):
        denom = 1.0
        if k > 0:
            denom = denom + couple[k - 1]
        if k < levels - 1:
            denom = denom + couple[k]
        if k > 0:
            denom = denom + couple[k - 1] * factor
        inverse = 1.0 / denom
        px, qx, py, qy = stencil[k]
        out.append(
            dict(
                centre=inverse * (1.0 - ((px - qx) + (py - qy))),
                west=inverse * px,
                east=inverse * qx,
                south=inverse * py,
                north=inverse * qy,
                lower=inverse * couple[k - 1] if k > 0 else None,
                upper=inverse * couple[k] if k < levels - 1 else None,
            )
        )
        factor = -out[k]["upper"] if k < levels - 1 else None
    return out


def solve_column(terms, cells):
    levels = len(terms)
    partial = []
    for k in range(levels):
        t = terms[k]
        base, west, east, south, north = cells(k)
        now = t["centre"] * base + (t["west"] * west - t["east"] * east) + (t["south"] * south - t["north"] * north)
        if k > 0:
            now = now + t["lower"] * partial[k - 1]
        partial.append(now)
    for k in range(levels - 2, -1, -1):
        partial[k] = partial[k] + terms[k]["upper"] * partial[k + 1]
    return partial


def kernel(
    sects,
    tiles,
    zonal_in,
    merid_in,
    height_in,
    sea_in,
    flags_in,
    conc_in,
    kappa_hbm,
    react_hbm,
    absorb_hbm,
    light_hbm,
    conc_out,
    zonal_out,
    merid_out,
    height_out,
    kappa_in,
    react_in,
    absorb_in,
    light_in,
    own,
    sea,
    flags,
    conc,
    react_d,
    base,
    west_v,
    east_v,
    south_v,
    north_v,
    cols_send,
    cols_recv,
    rows_send,
    rows_recv,
    blk_send,
    blk_recv,
    sea_send,
    sea_recv,
    mix_send,
    mix_recv,
    strip_send,
    strip_recv,
    wet_all,
    state,
    state_edge,
    means,
    last_means,
    force,
    out_send,
    out_recv,
    local_sem,
    blk_ssem,
    blk_rsem,
    sea_ssem,
    sea_rsem,
    mix_ssem,
    mix_rsem,
    state_ssem,
    state_rsem,
    force_ssem,
    force_rsem,
    strip_ssem,
    strip_rsem,
    halo_ssem,
    halo_rsem,
    out_ssem,
    out_rsem,
    known_sem,
):
    me_s = lax.axis_index("sect")
    me_t = lax.axis_index("tile")
    tracers, levels, rows, columns = conc_in.shape
    depth = zonal_in.shape[0]
    bands = 3
    far = bands

    def sect_at(offset):
        return lax.rem(me_s + (offset + sects), sects)

    def tile_at(offset):
        return lax.rem(me_t + (offset + tiles), tiles)

    def place(s, t):
        hops = t // 2
        for bit in range((sects - 1).bit_length()):
            hops = hops + lax.rem(s // (1 << bit), 2)
        return ((2 * hops + 1 - lax.rem(t, 2)) * tiles + t) * sects + s

    def across(m):
        s = me_s
        for bit in range((sects - 1).bit_length()):
            if m >> bit & 1:
                s = s + (1 << bit) - 2 * (1 << bit) * lax.rem(me_s // (1 << bit), 2)
        return s

    near = sorted(range(sects), key=lambda m: (m.bit_count(), m))
    peers = [(m, across(m), dt, tile_at(dt)) for dt in (1, 0, -1) for m in near if m or dt]
    mine = place(me_s, me_t)
    later, sooner, direct, answer = [], [], [], []
    for m, s, dt, t in peers:
        spot = place(s, t)
        later.append(spot > mine)
        sooner.append(spot < mine)
        if m and dt:
            direct.append(spot > place(me_s, t))
            answer.append((spot < mine) & (mine > place(s, me_t)))
        else:
            direct.append(True)
            answer.append(spot < mine)

    def remote(src, dst, send, recv, to_s, to_t):
        return pltpu.make_async_remote_copy(
            src_ref=src,
            dst_ref=dst,
            send_sem=send,
            recv_sem=recv,
            device_id=(to_s, to_t),
            device_id_type=pl.DeviceIdType.MESH,
        )

    fields_in = (zonal_in, merid_in, height_in)
    ocean_local = [pltpu.make_async_copy(field, own.at[f], local_sem.at[f]) for f, field in enumerate(fields_in)]
    ocean_local.append(pltpu.make_async_copy(sea_in, sea, local_sem.at[3]))
    tracer_local = [
        pltpu.make_async_copy(src, dst, local_sem.at[4 + i])
        for i, (src, dst) in enumerate(
            (
                (conc_in, conc),
                (flags_in, flags),
                (react_hbm, react_in),
                (absorb_hbm, absorb_in),
                (kappa_hbm, kappa_in),
                (light_hbm, light_in),
            )
        )
    ]
    barrier = pltpu.get_barrier_semaphore()
    @pl.when(me_t == 0)
    def _():
        for s in [across(m) for m in near[::-1]]:
            pl.semaphore_signal(barrier, inc=1, device_id=(s, tiles - 2), device_id_type=pl.DeviceIdType.MESH)

    heard = 0
    for n, (_, s, _, t) in reversed(list(enumerate(peers))):
        heard = heard + jnp.where(later[n], 0, 1)

        @pl.when(later[n])
        def _():
            pl.semaphore_signal(barrier, inc=1, device_id=(s, t), device_id_type=pl.DeviceIdType.MESH)

    for copy in ocean_local + tracer_local:
        copy.start()
    heard = heard + jnp.where(me_t == tiles - 2, sects, 0)

    @pl.when(heard > 0)
    def _():
        pl.semaphore_wait(barrier, heard)

    for n, (_, s, dt, t) in enumerate(peers):

        @pl.when(answer[n])
        def _():
            pl.semaphore_signal(
                known_sem.at[1 - dt, me_s], inc=1, device_id=(s, t), device_id_type=pl.DeviceIdType.MESH
            )

    lane = lax.broadcasted_iota(jnp.int32, (rows, columns), 1)
    row = lax.broadcasted_iota(jnp.int32, (rows, columns), 0)
    low_half = lane < LANES // 2

    for copy in ocean_local:
        copy.wait()

    def lanes_of(s):
        return slice((s % sects) * columns, (s % sects + 1) * columns)

    sea_f = [sea[:, lanes_of(s)].astype(jnp.float32) for s in range(sects)]
    for d in range(sects):
        for ld in range(depth):
            packed = None
            for f in range(4):
                if f < 3:
                    blk_send[d, 4 * ld + f] = own[f, ld, :, lanes_of(d)]
                    after, before = own[f, ld, :, lanes_of(d + 1)], own[f, ld, :, lanes_of(d - 1)]
                else:
                    after, before = sea_f[(d + 1) % sects], sea_f[(d - 1) % sects]
                edge = jnp.where(low_half, after, before)
                if f == 0:
                    packed = edge
                else:
                    inside = (lane >= 2 * EDGE * f - EDGE) & (lane < 2 * EDGE * f + EDGE)
                    packed = jnp.where(inside, pltpu.roll(edge, 2 * EDGE * f, 1), packed)
            blk_send[d, 4 * ld + 3] = packed
    own_columns = pl.ds(pl.multiple_of(me_s * columns, LANES), columns)
    wet_cols = sea[:, own_columns].astype(jnp.float32)
    is_wet = wet_cols == 1.0
    sea_send[...] = wet_cols

    def blk_copy(j, s_slot, send, to_s, to_t, src):
        return remote(blk_send.at[src], blk_recv.at[j, s_slot], send, blk_rsem.at[j, s_slot], to_s, to_t)

    sent = []
    to_peer = [
        blk_copy(1 - dt, me_s, blk_ssem.at[1 + dt, s], s, t, s) for _, s, dt, t in peers
    ]
    seas = [
        remote(sea_send, sea_recv.at[1 - dt], sea_ssem.at[1 + dt], sea_rsem.at[1 - dt], me_s, tile_at(dt))
        for dt in (1, -1)
    ]
    over = [blk_copy(far, me_s, blk_ssem.at[far, across(m)], across(m), 0, across(m)) for m in near[::-1]]
    over.append(remote(sea_send, sea_recv.at[far], sea_ssem.at[far], sea_rsem.at[far], me_s, 0))

    def begin(n):
        m, _, dt, _ = peers[n]
        if not m:
            seas[0 if dt == 1 else 1].start()
        to_peer[n].start()

    for n in sorted(range(len(peers)), key=lambda n: (-peers[n][2] % bands, -n)):

        @pl.when(sooner[n])
        def _():
            begin(n)

    @pl.when(me_t == tiles - 2)
    def _():
        for copy in over[sects:] + over[:sects]:
            copy.start()

    blk_recv[1, me_s] = blk_send[me_s]
    sea_recv[1] = sea_send[...]
    for copy in tracer_local:
        copy.wait()

    cells = tracers * levels

    def react_and_pack(turn, heated):
        names = tracers + (1 if heated else 0)
        to_east = [jnp.zeros((rows, columns), jnp.float32) for _ in range(pl.cdiv(cells, LANES))]
        to_west = list(to_east)
        for k in range(levels):
            old = [conc[i, k] for i in range(tracers)]
            heat_d = None
            for i in range(names):
                n = i * levels + k
                if i < tracers:
                    growth = react_in[i, 0] * old[0]
                    for j in range(1, tracers):
                        growth = growth + react_in[i, j] * old[j]
                    new = old[i] + tracer_step * growth
                    kept = jnp.where(is_wet, new, old[i])
                    if heated:
                        a = absorb_in[i]
                        heat_d = a * new if i == 0 else heat_d + a * new
                        heat_b = a * kept if i == 0 else heat_b + a * kept
                else:
                    mix_send[k] = heat_d
                    mix_send[levels + k] = heat_b
                    rows_send[turn, 0, pl.ds(n, 1)] = heat_d[rows - 1 : rows]
                    rows_send[turn, 1, pl.ds(n, 1)] = heat_d[0:1]
                    continue
                react_d[n] = new
                base[n] = kept
                rows_send[turn, 0, pl.ds(n, 1)] = new[rows - 1 : rows]
                rows_send[turn, 1, pl.ds(n, 1)] = new[0:1]
                p, at = divmod(n, LANES)
                here = lane == at
                turned = pltpu.roll(new, (at + 1) % columns, 1)
                to_east[p] = jnp.where(here, turned, to_east[p])
                turned = pltpu.roll(new, at, 1) if at else new
                to_west[p] = jnp.where(here, turned, to_west[p])
        for p in range(len(to_east)):
            cols_send[turn, 0, p] = to_east[p]
            cols_send[turn, 1, p] = to_west[p]
        return halo_copies(turn, names * levels)

    def halo_copies(turn, count):
        tall = pl.cdiv(count, 8) * 8
        copies = []
        for i, d in enumerate((1, -1)):
            copies.append(
                remote(
                    rows_send.at[turn, i, pl.ds(0, tall)],
                    rows_recv.at[turn, i, pl.ds(0, tall)],
                    halo_ssem.at[turn, i],
                    halo_rsem.at[turn, i],
                    me_s,
                    tile_at(d),
                )
            )
            copies.append(
                remote(
                    cols_send.at[turn, i],
                    cols_recv.at[turn, i],
                    halo_ssem.at[turn, 2 + i],
                    halo_rsem.at[turn, 2 + i],
                    sect_at(d),
                    me_t,
                )
            )
        return copies

    def shift_cells(turn):
        from_west = [cols_recv[turn, 0, p] for p in range(pl.cdiv(cells, LANES))]
        from_east = [cols_recv[turn, 1, p] for p in range(pl.cdiv(cells, LANES))]
        for n in range(cells):
            p, at = divmod(n, LANES)
            new = react_d[n]
            edge = pltpu.roll(from_west[p], columns - at, 1) if at else from_west[p]
            west_v[n] = jnp.where(lane == 0, edge, pltpu.roll(new, 1, 1))
            edge = pltpu.roll(from_east[p], columns - 1 - at, 1) if at < columns - 1 else from_east[p]
            east_v[n] = jnp.where(lane == columns - 1, edge, pltpu.roll(new, columns - 1, 1))
            edge = jnp.broadcast_to(rows_recv[turn, 0, pl.ds(n, 1)], (rows, columns))
            south_v[n] = jnp.where(row == 0, edge, pltpu.roll(new, 1, 0))
            edge = jnp.broadcast_to(rows_recv[turn, 1, pl.ds(n, 1)], (rows, columns))
            north_v[n] = jnp.where(row == rows - 1, edge, pltpu.roll(new, rows - 1, 0))

    def tracer_cells(i):
        def read(k):
            n = i * levels + k
            return base[n], west_v[n], east_v[n], south_v[n], north_v[n]

        return read

    halo0 = react_and_pack(0, True)
    for k in range(levels):
        mix_send[2 * levels + k] = flags[k].astype(jnp.float32)
    per = LANES // NEAR
    for p in range(pl.cdiv(3 * levels, per)):
        to_east = to_west = jnp.zeros((rows, columns), jnp.float32)
        for at in range(min(per, 3 * levels - p * per)):
            value = mix_send[p * per + at]
            here = (lane >= NEAR * at) & (lane < NEAR * at + NEAR)
            turned = pltpu.roll(value, (NEAR * at + NEAR) % LANES, 1)
            to_east = jnp.where(here, turned, to_east)
            turned = pltpu.roll(value, NEAR * at, 1) if at else value
            to_west = jnp.where(here, turned, to_west)
        strip_send[0, p] = to_east
        strip_send[1, p] = to_west
    sent.extend(seas)
    strips = []
    for i, ds in enumerate((1, -1)):
        for dt in (1, -1, 0):
            strips.append(
                remote(
                    strip_send.at[i],
                    strip_recv.at[i, 1 - dt],
                    strip_ssem.at[i, 1 - dt],
                    strip_rsem.at[i, 1 - dt],
                    sect_at(ds),
                    tile_at(dt),
                )
            )
    sent.extend(strips + halo0)

    def reach(n, when):
        _, s, dt, _ = peers[n]

        @pl.when(later[n] & when)
        def _():
            @pl.when(direct[n])
            def _():
                pl.semaphore_wait(known_sem.at[1 + dt, s], 1)

            begin(n)

    def edges(dt):
        if dt:
            halo0[0 if dt == 1 else 2].start()
        else:
            halo0[1].start()
            halo0[3].start()
        for i in range(2):
            strips[3 * i + (1, -1, 0).index(dt)].start()

    ready = {}
    for dt in (1, -1, 0):
        ready[dt] = True
        for ds in (0, 1, -1):
            if ds or dt:
                ready[dt] = (place(sect_at(ds), tile_at(dt)) < mine) & ready[dt]

        @pl.when(ready[dt])
        def _():
            edges(dt)

    for n in sorted(range(len(peers)), key=lambda n: (near.index(peers[n][0]), n)):
        reach(n, me_t != 0 if peers[n][2] == -1 else True)
    for dt in (0, 1):

        @pl.when(jnp.logical_not(ready[dt]))
        def _():
            edges(dt)

    for n, peer in enumerate(peers):
        if peer[2] == -1:
            reach(n, me_t == 0)

    @pl.when(jnp.logical_not(ready[-1]))
    def _():
        edges(-1)

    rest = remote(mix_send, mix_recv, mix_ssem.at[0], mix_rsem.at[0], me_s, 0)

    @pl.when(me_t == tiles - 1)
    def _():
        rest.start()


    for copy in seas:
        copy.wait_recv()

    def blk_wait(j, s):
        blk_copy(j, s, blk_ssem.at[0, 0], me_s, me_t, me_s).wait_recv()

    for j in (0, 2):
        blk_wait(j, me_s)
    in_edge = (lane < EDGE) | (lane >= LANES - EDGE)

    def wet_band(j):
        turned = pltpu.roll(blk_recv[j, me_s, 3], LANES - 6 * EDGE, 1)
        return jnp.concatenate([sea_recv[j], jnp.where(in_edge, turned, 0.0)], axis=1)

    for j in range(bands):
        wet_all[j * rows : (j + 1) * rows] = wet_band(j)
    centre = slice(rows, 2 * rows)

    def first_levels(group, slots, wet, target):
        for l in [group * FIRST * depth + ld for ld in range(FIRST * depth)]:
            s, ld = l // depth, lax.rem(l, depth)
            full = []
            packed = [blk_recv[j, s, 4 * ld + 3] for j in slots]
            for f in range(3):
                parts = []
                for j, pack in zip(slots, packed):
                    turned = pltpu.roll(pack, LANES - 2 * EDGE * f, 1) if f else pack
                    parts.append(jnp.concatenate([blk_recv[j, s, 4 * ld + f], turned], axis=1))
                full.append(jnp.concatenate(parts, axis=0))
            z, m, h, zm, mm = ocean_steps(*full, wet, None, (centre, slice(None)))
            for f, value in enumerate((z, m, h)):
                state[target, 3 * l + f] = value[:, 0:columns]
                state_edge[target, 3 * l + f] = value[:, columns:]
            for i, value in enumerate((zm, mm)):
                means[target, l, i] = value

    def first_interval(group, carry):
        for s in [group * FIRST + at for at in range(FIRST)]:

            @pl.when(s != me_s)
            def _():
                for j in range(bands):
                    blk_wait(j, s)

        first_levels(group, (0, 1, 2), wet_all[...], 1)
        return carry

    def beyond_interval(group, carry):
        for at in range(FIRST):
            blk_wait(far, group * FIRST + at)
        first_levels(group, (far, 0, 1), jnp.concatenate([wet_band(far), wet_all[0 : 2 * rows]], axis=0), 0)
        return carry

    lax.fori_loop(0, sects // FIRST, first_interval, 0)

    pair = LANES // (2 * NEAR)

    def pack_edges(buffer, slot, values):
        start = buffer.shape[1] - pl.cdiv(len(values), pair)
        for p in range(pl.cdiv(len(values), pair)):
            tile = values[p * pair]
            for i, value in enumerate(values[p * pair + 1 : (p + 1) * pair], 1):
                here = (lane >= 2 * NEAR * i - NEAR) & (lane < 2 * NEAR * i + NEAR)
                tile = jnp.where(here, pltpu.roll(value, 2 * NEAR * i, 1), tile)
            buffer[slot, start + p] = tile

    def with_edges(buffer, slot, q, count):
        start = buffer.shape[1] - pl.cdiv(count, pair)
        p, at = divmod(q, pair)
        edge = buffer[slot, start + p]
        if at:
            edge = pltpu.roll(edge, LANES - 2 * NEAR * at, 1)
        return jnp.concatenate([buffer[slot, q], edge], axis=1)

    pack_edges(state, 1, [state_edge[1, q] for q in range(3 * levels)])

    def neighbours(buffer, send, recv):
        return [
            remote(buffer.at[1], buffer.at[0], send.at[0], recv.at[0], me_s, tile_at(1)),
            remote(buffer.at[1], buffer.at[2], send.at[1], recv.at[1], me_s, tile_at(-1)),
        ]

    states = neighbours(state, state_ssem, state_rsem)
    forces = neighbours(force, force_ssem, force_rsem)

    def hand_on(copies):
        copies[1].start()

        @pl.when(me_t != tiles - 1)
        def _():
            copies[0].start()

    hand_on(states)
    half_wet = tracer_step * wet_cols

    def first_tracers():
        upwind = [flags[k] == 1 for k in range(levels)]
        speeds = [tuple(means[1, k, i, :, 0:columns] for i in range(2)) for k in range(levels)]
        terms = column_terms(speeds, upwind, half_wet, kappa_in)
        shift_cells(0)
        for i in range(tracers):
            for k, value in enumerate(solve_column(terms, tracer_cells(i))):
                conc[i, k] = value
        for copy in react_and_pack(1, False):
            copy.start()

    halo1 = halo_copies(1, cells)
    sent.extend(halo1)
    for copy in halo0:
        copy.wait_recv()

    @pl.when(me_t == 0)
    def _():
        first_tracers()

    for copy in strips:
        copy.wait_recv()

    def halo_tile(q, j):
        p, at = divmod(q, per)
        west_part = pltpu.roll(strip_recv[0, j, p], LANES - NEAR - NEAR * at, 1)
        east_part = strip_recv[1, j, p]
        if at:
            east_part = pltpu.roll(east_part, LANES - NEAR * at, 1)
        return jnp.where(low_half, east_part, west_part)

    def wide_tile(q, j):
        return jnp.concatenate([mix_send[q] if j == 1 else mix_recv[q], halo_tile(q, j)], axis=1)

    wide = columns + LANES

    def heat_band(j):
        speeds = [(means[j, k, 0], means[j, k, 1]) for k in range(levels)]
        upwind = [wide_tile(2 * levels + k, j) > 0.5 for k in range(levels)]
        terms = column_terms(speeds, upwind, tracer_step * wet_all[j * rows : (j + 1) * rows], kappa_in)
        first = lax.broadcasted_iota(jnp.int32, (rows, wide), 0) == 0
        last = lax.broadcasted_iota(jnp.int32, (rows, wide), 0) == rows - 1

        def row_beside(k, i, side):
            at = slice(rows - 1, rows) if i == 0 else slice(0, 1)
            if i == 1:
                return wide_tile(k, 1)[at]
            return jnp.concatenate([rows_recv[0, side, pl.ds(cells + k, 1)], halo_tile(k, i)[at]], axis=1)

        def heat_cells(k):
            d = wide_tile(k, j)
            south, north = pltpu.roll(d, 1, 0), pltpu.roll(d, rows - 1, 0)
            if j == 1:
                south = jnp.where(first, jnp.broadcast_to(row_beside(k, 0, 0), d.shape), south)
            north = jnp.where(last, jnp.broadcast_to(row_beside(k, j + 1, 1), d.shape), north)
            return wide_tile(levels + k, j), pltpu.roll(d, 1, 1), pltpu.roll(d, wide - 1, 1), south, north

        edges = []
        for k, value in enumerate(solve_column(terms, heat_cells)):
            value = (time_step * heat_coupling) * (light_in[k] * value)
            force[j, k] = value[:, 0:columns]
            edges.append(value[:, columns:])
        pack_edges(force, j, edges)

    heat_band(1)
    hand_on(forces)

    @pl.when(me_t != 0)
    def _():
        first_tracers()

    @pl.when(me_t == 0)
    def _():
        over[sects].wait_recv()
        lax.fori_loop(0, sects // FIRST, beyond_interval, 0)
        pack_edges(state, 0, [state_edge[0, q] for q in range(3 * levels)])
        rest.wait_recv()
        heat_band(0)

    states[1].wait_recv()
    forces[1].wait_recv()

    @pl.when(me_t != 0)
    def _():
        states[0].wait_recv()
        forces[0].wait_recv()

    def out_copy(l):
        owner, ld = l // depth, l % depth
        return remote(
            out_send.at[l], out_recv.at[me_s, ld], out_ssem.at[l], out_rsem.at[me_s, ld], owner, me_t
        )

    def second_interval(group):
        for l in [group * SECOND + at for at in range(SECOND)]:
            whole = [
                jnp.concatenate([with_edges(state, j, 3 * l + f, 3 * levels) for j in range(bands)], axis=0)
                for f in range(3)
            ]
            forced = jnp.concatenate([with_edges(force, j, l, levels) for j in range(bands)], axis=0)
            z, m, h, zm, mm = ocean_steps(*whole, wet_all[...], forced, (centre, slice(0, columns)))
            last_means[l, 0] = zm
            last_means[l, 1] = mm
            for f, value in enumerate((z, m, h)):
                out_send[l, f] = value
        for l in [group * SECOND + at for at in range(SECOND)]:

            @pl.when(l // depth != me_s)
            def _():
                out_copy(l).start()

    for group in range(levels // SECOND):
        second_interval(group)
    for ld in range(depth):
        out_recv[me_s, ld] = out_send[me_s * depth + ld]

    upwind = [flags[k] == 1 for k in range(levels)]
    speeds = [(last_means[k, 0], last_means[k, 1]) for k in range(levels)]
    terms = column_terms(speeds, upwind, half_wet, kappa_in)
    for copy in halo1:
        copy.wait_recv()
    shift_cells(1)
    for i in range(tracers):
        for k, value in enumerate(solve_column(terms, tracer_cells(i))):
            conc_out[i, k] = value

    def gather(s, carry):
        @pl.when(s != me_s)
        def _():
            for ld in range(depth):
                remote(
                    out_send.at[0], out_recv.at[s, ld], out_ssem.at[0], out_rsem.at[s, ld], me_s, me_t
                ).wait_recv()

        return carry

    lax.fori_loop(0, sects, gather, 0)
    for s in range(sects):
        for ld in range(depth):
            for f, ref in enumerate((zonal_out, merid_out, height_out)):
                ref[ld, :, lanes_of(s)] = out_recv[s, ld, f]
    for copy in sent + [states[1], forces[1]]:
        copy.wait_send()

    for copy in to_peer:
        copy.wait_send()

    @pl.when(me_t != tiles - 1)
    def _():
        states[0].wait_send()
        forces[0].wait_send()

    @pl.when(me_t == tiles - 1)
    def _():
        rest.wait_send()

    @pl.when(me_t == tiles - 2)
    def _():
        for copy in over:
            copy.wait_send()


    def drain(l, carry):
        @pl.when(l // depth != me_s)
        def _():
            out_copy(l).wait_send()

        return carry

    lax.fori_loop(0, levels, drain, 0)


def put_out(*refs):
    copies = [
        pltpu.make_async_copy(src, dst, refs[8].at[i])
        for i, (src, dst) in enumerate(zip(refs[:4], refs[4:8]))
    ]
    for copy in copies:
        copy.start()
    for copy in copies:
        copy.wait()


def body(sects, tiles, zonal, merid, height, level_kappa, sea, flags, conc, react, absorb, light):
    tracers, levels, rows, columns = conc.shape
    depth, _, wide = zonal.shape
    assert rows >= NEAR and columns == LANES and INTERVALS == 2
    assert tiles > 3 and sects > 1 and levels == sects * depth and wide == sects * columns
    cells = tracers * levels
    packs = pl.cdiv(cells, LANES)
    padded = pl.cdiv(cells + levels, 8) * 8
    strips = pl.cdiv(3 * levels, LANES // NEAR)
    pair = LANES // (2 * NEAR)
    f32 = jnp.float32
    dma = pltpu.SemaphoreType.DMA
    any_space = pl.BlockSpec(memory_space=pl.ANY)
    vmem = pl.BlockSpec(memory_space=pltpu.VMEM)
    results = pl.pallas_call(
        functools.partial(kernel, sects, tiles),
        out_shape=[
            pltpu.VMEM(conc.shape, f32),
            pltpu.VMEM(zonal.shape, f32),
            pltpu.VMEM(merid.shape, f32),
            pltpu.VMEM(height.shape, f32),
        ],
        in_specs=[pl.BlockSpec(memory_space=pltpu.HBM)] * 10,
        out_specs=[vmem] * 4,
        scratch_shapes=[
            pltpu.SMEM(level_kappa.shape, f32),
            pltpu.SMEM(react.shape, f32),
            pltpu.SMEM(absorb.shape, f32),
            pltpu.SMEM(light.shape, f32),
            pltpu.VMEM((3, depth, rows, wide), f32),
            pltpu.VMEM((rows, wide), jnp.int32),
            pltpu.VMEM(flags.shape, jnp.int32),
            pltpu.VMEM(conc.shape, f32),
        ]
        + [pltpu.VMEM((cells, rows, columns), f32)] * 6
        + [
            pltpu.VMEM((2, 2, packs, rows, columns), f32),
            pltpu.VMEM((2, 2, packs, rows, columns), f32),
            pltpu.VMEM((2, 2, padded, columns), f32),
            pltpu.VMEM((2, 2, padded, columns), f32),
            pltpu.VMEM((sects, 4 * depth, rows, columns), f32),
            pltpu.VMEM((4, sects, 4 * depth, rows, columns), f32),
            pltpu.VMEM((rows, columns), f32),
            pltpu.VMEM((4, rows, columns), f32),
            pltpu.VMEM((3 * levels, rows, columns), f32),
            pltpu.VMEM((3 * levels, rows, columns), f32),
            pltpu.VMEM((2, strips, rows, columns), f32),
            pltpu.VMEM((2, 3, strips, rows, columns), f32),
            pltpu.VMEM((3 * rows, columns + LANES), f32),
            pltpu.VMEM((3, 3 * levels + pl.cdiv(3 * levels, pair), rows, columns), f32),
            pltpu.VMEM((2, 3 * levels, rows, columns), f32),
            pltpu.VMEM((2, levels, 2, rows, columns + LANES), f32),
            pltpu.VMEM((levels, 2, rows, columns), f32),
            pltpu.VMEM((3, levels + pl.cdiv(levels, pair), rows, columns), f32),
            pltpu.VMEM((levels, 3, rows, columns), f32),
            pltpu.VMEM((sects, depth, 3, rows, columns), f32),
            dma((10,)),
            dma((4, sects)),
            dma((4, sects)),
            dma((4,)),
            dma((4,)),
            dma((1,)),
            dma((1,)),
            dma((2,)),
            dma((2,)),
            dma((2,)),
            dma((2,)),
            dma((2, 3)),
            dma((2, 3)),
            dma((2, 4)),
            dma((2, 4)),
            dma((levels,)),
            dma((sects, depth)),
            pltpu.SemaphoreType.REGULAR((3, sects)),
        ],
        compiler_params=pltpu.CompilerParams(collective_id=0, has_side_effects=True),
        name="coupled",
    )(zonal, merid, height, sea, flags, conc, level_kappa, react, absorb, light)
    return pl.pallas_call(
        put_out,
        out_shape=[jax.ShapeDtypeStruct(r.shape, f32) for r in results],
        in_specs=[vmem] * 4,
        out_specs=[any_space] * 4,
        scratch_shapes=[dma((4,))],
        name="put_out",
    )(*[pltpu.with_memory_space_constraint(r, pltpu.VMEM) for r in results])


def solution(mesh):
    placed = (
        P("sect", "tile", None),
        P("sect", "tile", None),
        P("sect", "tile", None),
        P(),
        P("tile", None),
        P(None, "tile", "sect"),
        P(None, None, "tile", "sect"),
        P(),
        P(),
        P(),
    )
    return jax.shard_map(
        functools.partial(body, mesh.shape["sect"], mesh.shape["tile"]),
        mesh=mesh,
        in_specs=placed,
        out_specs=(
            P(None, None, "tile", "sect"),
            P("sect", "tile", None),
            P("sect", "tile", None),
            P("sect", "tile", None),
        ),
        check_vma=False,
    )
```

```python
import functools

import jax
import jax.numpy as jnp
from jax import lax
from jax.experimental import pallas as pl
from jax.experimental.pallas import tpu as pltpu
from jax.sharding import PartitionSpec as P

STEPS = 4
INTERVALS = 2

time_step = 0.1
gravity = 1.0
coriolis = 0.3
viscosity = 0.05
heat_coupling = 0.05
tracer_step = 0.5
stir_gain = 4.0

LANES = 128
EDGE = 4 * STEPS
NEAR = EDGE // 2
FIRST = 4
SECOND = 2


def ocean_steps(zonal, merid, height, wet, forced, keep):
    tall, wide = zonal.shape

    def east(a):
        return pltpu.roll(a, wide - 1, 1)

    def west(a):
        return pltpu.roll(a, 1, 1)

    def north(a):
        return pltpu.roll(a, tall - 1, 0)

    def south(a):
        return pltpu.roll(a, 1, 0)

    keep_rate = time_step * viscosity
    self_rate = 1.0 / keep_rate - 4.0
    turn_rate = time_step * coriolis / keep_rate
    steep = 0.5 * gravity * time_step / keep_rate
    gain = keep_rate * wet
    rise = steep * height
    if forced is not None:
        forced = steep * forced
    zonal_sum = merid_sum = None
    for step in range(STEPS):
        ze, zw, zn, zs = east(zonal), west(zonal), north(zonal), south(zonal)
        me, mw, mn, ms = east(merid), west(merid), north(merid), south(merid)
        rise = rise - (0.5 * time_step * steep) * ((ze - zw) + (mn - ms))
        zonal_part = ((ze + zw) + (zn + zs)) + (self_rate * zonal + turn_rate * merid)
        merid_part = ((me + mw) + (mn + ms)) + (self_rate * merid - turn_rate * zonal)
        if forced is not None:
            rise = rise + forced
        zonal_new = gain * (zonal_part - (east(rise) - west(rise)))
        merid_new = gain * (merid_part - (north(rise) - south(rise)))
        zonal, merid = zonal_new, merid_new
        zonal_sum = zonal[keep] if step == 0 else zonal_sum + zonal[keep]
        merid_sum = merid[keep] if step == 0 else merid_sum + merid[keep]
    return zonal[keep], merid[keep], (1.0 / steep) * rise[keep], zonal_sum / STEPS, merid_sum / STEPS


def column_terms(speeds, upwind, half_wet, kappa_in):
    levels = len(speeds)
    kappa, stencil = [], []
    for k in range(levels):
        along_x, along_y = speeds[k]
        kappa.append(kappa_in[k] * (1.0 + stir_gain * (along_x * along_x + along_y * along_y)))
        terms = []
        for speed in (along_x, along_y):
            terms.append(half_wet * jnp.where(upwind[k], jnp.maximum(speed, 0.0), 0.5 * speed))
            terms.append(half_wet * jnp.where(upwind[k], jnp.minimum(speed, 0.0), 0.5 * speed))
        stencil.append(terms)
    couple = [tracer_step * 0.5 * (kappa[k] + kappa[k + 1]) for k in range(levels - 1)]
    out, factor = [], None
    for k in range(levels):
        denom = 1.0
        if k > 0:
            denom = denom + couple[k - 1]
        if k < levels - 1:
            denom = denom + couple[k]
        if k > 0:
            denom = denom + couple[k - 1] * factor
        inverse = 1.0 / denom
        px, qx, py, qy = stencil[k]
        out.append(
            dict(
                centre=inverse * (1.0 - ((px - qx) + (py - qy))),
                west=inverse * px,
                east=inverse * qx,
                south=inverse * py,
                north=inverse * qy,
                lower=inverse * couple[k - 1] if k > 0 else None,
                upper=inverse * couple[k] if k < levels - 1 else None,
            )
        )
        factor = -out[k]["upper"] if k < levels - 1 else None
    return out


def solve_column(terms, cells):
    levels = len(terms)
    partial = []
    for k in range(levels):
        t = terms[k]
        base, west, east, south, north = cells(k)
        now = t["centre"] * base + (t["west"] * west - t["east"] * east) + (t["south"] * south - t["north"] * north)
        if k > 0:
            now = now + t["lower"] * partial[k - 1]
        partial.append(now)
    for k in range(levels - 2, -1, -1):
        partial[k] = partial[k] + terms[k]["upper"] * partial[k + 1]
    return partial


def kernel(
    sects,
    tiles,
    zonal_in,
    merid_in,
    height_in,
    sea_in,
    flags_in,
    conc_in,
    kappa_hbm,
    react_hbm,
    absorb_hbm,
    light_hbm,
    conc_out,
    zonal_out,
    merid_out,
    height_out,
    kappa_in,
    react_in,
    absorb_in,
    light_in,
    own,
    sea,
    flags,
    conc,
    react_d,
    base,
    west_v,
    east_v,
    south_v,
    north_v,
    cols_send,
    cols_recv,
    rows_send,
    rows_recv,
    blk_send,
    blk_recv,
    sea_send,
    sea_recv,
    mix_send,
    mix_recv,
    strip_send,
    strip_recv,
    wet_all,
    state,
    state_edge,
    means,
    last_means,
    force,
    out_send,
    out_recv,
    local_sem,
    blk_ssem,
    blk_rsem,
    sea_ssem,
    sea_rsem,
    mix_ssem,
    mix_rsem,
    state_ssem,
    state_rsem,
    force_ssem,
    force_rsem,
    strip_ssem,
    strip_rsem,
    halo_ssem,
    halo_rsem,
    out_ssem,
    out_rsem,
    known_sem,
):
    me_s = lax.axis_index("sect")
    me_t = lax.axis_index("tile")
    tracers, levels, rows, columns = conc_in.shape
    depth = zonal_in.shape[0]
    bands = 3
    far = bands

    def sect_at(offset):
        return lax.rem(me_s + (offset + sects), sects)

    def tile_at(offset):
        return lax.rem(me_t + (offset + tiles), tiles)

    def place(s, t):
        hops = t // 2
        for bit in range((sects - 1).bit_length()):
            hops = hops + lax.rem(s // (1 << bit), 2)
        return ((2 * hops + 1 - lax.rem(t, 2)) * tiles + t) * sects + s

    def across(m):
        s = me_s
        for bit in range((sects - 1).bit_length()):
            if m >> bit & 1:
                s = s + (1 << bit) - 2 * (1 << bit) * lax.rem(me_s // (1 << bit), 2)
        return s

    near = sorted(range(sects), key=lambda m: (m.bit_count(), m))
    peers = [(m, across(m), dt, tile_at(dt)) for dt in (1, 0, -1) for m in near if m or dt]
    bits = [lax.rem(me_s // (1 << bit), 2) for bit in range((sects - 1).bit_length())]
    rows_of = {dt: (2 * (t // 2) + 1 - lax.rem(t, 2), t) for dt, t in ((dt, tile_at(dt)) for dt in (1, 0, -1))}
    hops_of = {m: sum((1 - b if m >> i & 1 else b) for i, b in enumerate(bits)) for m in near}
    spots = {
        (m, dt): ((2 * hops_of[m] + rows_of[dt][0]) * tiles + rows_of[dt][1]) * sects + across(m)
        for m in near
        for dt in (1, 0, -1)
    }
    mine = spots[0, 0]
    later, sooner, direct, answer = [], [], [], []
    for m, s, dt, t in peers:
        spot = spots[m, dt]
        later.append(spot > mine)
        sooner.append(spot < mine)
        if m and dt:
            direct.append(spot > spots[0, dt])
            answer.append((spot < mine) & (mine > spots[m, 0]))
        else:
            direct.append(True)
            answer.append(spot < mine)

    def remote(src, dst, send, recv, to_s, to_t):
        return pltpu.make_async_remote_copy(
            src_ref=src,
            dst_ref=dst,
            send_sem=send,
            recv_sem=recv,
            device_id=(to_s, to_t),
            device_id_type=pl.DeviceIdType.MESH,
        )

    fields_in = (zonal_in, merid_in, height_in)
    ocean_local = [pltpu.make_async_copy(field, own.at[f], local_sem.at[f]) for f, field in enumerate(fields_in)]
    ocean_local.append(pltpu.make_async_copy(sea_in, sea, local_sem.at[3]))
    tracer_local = [
        pltpu.make_async_copy(src, dst, local_sem.at[4 + i])
        for i, (src, dst) in enumerate(
            (
                (conc_in, conc),
                (flags_in, flags),
                (react_hbm, react_in),
                (absorb_hbm, absorb_in),
                (kappa_hbm, kappa_in),
                (light_hbm, light_in),
            )
        )
    ]
    barrier = pltpu.get_barrier_semaphore()
    @pl.when(me_t == 0)
    def _():
        for s in [across(m) for m in near[::-1]]:
            pl.semaphore_signal(barrier, inc=1, device_id=(s, tiles - 2), device_id_type=pl.DeviceIdType.MESH)

    heard = 0
    for n, (_, s, _, t) in reversed(list(enumerate(peers))):
        heard = heard + jnp.where(later[n], 0, 1)

        @pl.when(later[n])
        def _():
            pl.semaphore_signal(barrier, inc=1, device_id=(s, t), device_id_type=pl.DeviceIdType.MESH)

    for copy in ocean_local + tracer_local:
        copy.start()
    heard = heard + jnp.where(me_t == tiles - 2, sects, 0)

    @pl.when(heard > 0)
    def _():
        pl.semaphore_wait(barrier, heard)

    for n, (_, s, dt, t) in enumerate(peers):

        @pl.when(answer[n])
        def _():
            pl.semaphore_signal(
                known_sem.at[1 - dt, me_s], inc=1, device_id=(s, t), device_id_type=pl.DeviceIdType.MESH
            )

    lane = lax.broadcasted_iota(jnp.int32, (rows, columns), 1)
    row = lax.broadcasted_iota(jnp.int32, (rows, columns), 0)
    low_half = lane < LANES // 2

    for copy in ocean_local:
        copy.wait()

    def lanes_of(s):
        return slice((s % sects) * columns, (s % sects + 1) * columns)

    sea_f = [sea[:, lanes_of(s)].astype(jnp.float32) for s in range(sects)]
    for d in range(sects):
        for ld in range(depth):
            packed = None
            for f in range(4):
                if f < 3:
                    blk_send[d, 4 * ld + f] = own[f, ld, :, lanes_of(d)]
                    after, before = own[f, ld, :, lanes_of(d + 1)], own[f, ld, :, lanes_of(d - 1)]
                else:
                    after, before = sea_f[(d + 1) % sects], sea_f[(d - 1) % sects]
                edge = jnp.where(low_half, after, before)
                if f == 0:
                    packed = edge
                else:
                    inside = (lane >= 2 * EDGE * f - EDGE) & (lane < 2 * EDGE * f + EDGE)
                    packed = jnp.where(inside, pltpu.roll(edge, 2 * EDGE * f, 1), packed)
            blk_send[d, 4 * ld + 3] = packed
    own_columns = pl.ds(pl.multiple_of(me_s * columns, LANES), columns)
    wet_cols = sea[:, own_columns].astype(jnp.float32)
    is_wet = wet_cols == 1.0
    sea_send[...] = wet_cols

    def blk_copy(j, s_slot, send, to_s, to_t, src):
        return remote(blk_send.at[src], blk_recv.at[j, s_slot], send, blk_rsem.at[j, s_slot], to_s, to_t)

    sent = []
    to_peer = [
        blk_copy(1 - dt, me_s, blk_ssem.at[1 + dt, s], s, t, s) for _, s, dt, t in peers
    ]
    seas = [
        remote(sea_send, sea_recv.at[1 - dt], sea_ssem.at[1 + dt], sea_rsem.at[1 - dt], me_s, tile_at(dt))
        for dt in (1, -1)
    ]
    over = [blk_copy(far, me_s, blk_ssem.at[far, across(m)], across(m), 0, across(m)) for m in near[::-1]]
    over.append(remote(sea_send, sea_recv.at[far], sea_ssem.at[far], sea_rsem.at[far], me_s, 0))

    def begin(n):
        m, _, dt, _ = peers[n]
        if not m:
            seas[0 if dt == 1 else 1].start()
        to_peer[n].start()

    for n in sorted(range(len(peers)), key=lambda n: (-peers[n][2] % bands, -n)):

        @pl.when(sooner[n])
        def _():
            begin(n)

    @pl.when(me_t == tiles - 2)
    def _():
        for copy in over[sects:] + over[:sects]:
            copy.start()

    blk_recv[1, me_s] = blk_send[me_s]
    sea_recv[1] = sea_send[...]
    for copy in tracer_local:
        copy.wait()

    cells = tracers * levels

    def react_and_pack(turn, heated):
        names = tracers + (1 if heated else 0)
        to_east = [jnp.zeros((rows, columns), jnp.float32) for _ in range(pl.cdiv(cells, LANES))]
        to_west = list(to_east)
        for k in range(levels):
            old = [conc[i, k] for i in range(tracers)]
            heat_d = None
            for i in range(names):
                n = i * levels + k
                if i < tracers:
                    growth = react_in[i, 0] * old[0]
                    for j in range(1, tracers):
                        growth = growth + react_in[i, j] * old[j]
                    new = old[i] + tracer_step * growth
                    kept = jnp.where(is_wet, new, old[i])
                    if heated:
                        a = absorb_in[i]
                        heat_d = a * new if i == 0 else heat_d + a * new
                        heat_b = a * kept if i == 0 else heat_b + a * kept
                else:
                    mix_send[k] = heat_d
                    mix_send[levels + k] = heat_b
                    rows_send[turn, 0, pl.ds(n, 1)] = heat_d[rows - 1 : rows]
                    rows_send[turn, 1, pl.ds(n, 1)] = heat_d[0:1]
                    continue
                react_d[n] = new
                base[n] = kept
                rows_send[turn, 0, pl.ds(n, 1)] = new[rows - 1 : rows]
                rows_send[turn, 1, pl.ds(n, 1)] = new[0:1]
                p, at = divmod(n, LANES)
                here = lane == at
                turned = pltpu.roll(new, (at + 1) % columns, 1)
                to_east[p] = jnp.where(here, turned, to_east[p])
                turned = pltpu.roll(new, at, 1) if at else new
                to_west[p] = jnp.where(here, turned, to_west[p])
        for p in range(len(to_east)):
            cols_send[turn, 0, p] = to_east[p]
            cols_send[turn, 1, p] = to_west[p]
        return halo_copies(turn, names * levels)

    def halo_copies(turn, count):
        tall = pl.cdiv(count, 8) * 8
        copies = []
        for i, d in enumerate((1, -1)):
            copies.append(
                remote(
                    rows_send.at[turn, i, pl.ds(0, tall)],
                    rows_recv.at[turn, i, pl.ds(0, tall)],
                    halo_ssem.at[turn, i],
                    halo_rsem.at[turn, i],
                    me_s,
                    tile_at(d),
                )
            )
            copies.append(
                remote(
                    cols_send.at[turn, i],
                    cols_recv.at[turn, i],
                    halo_ssem.at[turn, 2 + i],
                    halo_rsem.at[turn, 2 + i],
                    sect_at(d),
                    me_t,
                )
            )
        return copies

    def shift_cells(turn):
        from_west = [cols_recv[turn, 0, p] for p in range(pl.cdiv(cells, LANES))]
        from_east = [cols_recv[turn, 1, p] for p in range(pl.cdiv(cells, LANES))]
        for n in range(cells):
            p, at = divmod(n, LANES)
            new = react_d[n]
            edge = pltpu.roll(from_west[p], columns - at, 1) if at else from_west[p]
            west_v[n] = jnp.where(lane == 0, edge, pltpu.roll(new, 1, 1))
            edge = pltpu.roll(from_east[p], columns - 1 - at, 1) if at < columns - 1 else from_east[p]
            east_v[n] = jnp.where(lane == columns - 1, edge, pltpu.roll(new, columns - 1, 1))
            edge = jnp.broadcast_to(rows_recv[turn, 0, pl.ds(n, 1)], (rows, columns))
            south_v[n] = jnp.where(row == 0, edge, pltpu.roll(new, 1, 0))
            edge = jnp.broadcast_to(rows_recv[turn, 1, pl.ds(n, 1)], (rows, columns))
            north_v[n] = jnp.where(row == rows - 1, edge, pltpu.roll(new, rows - 1, 0))

    def tracer_cells(i):
        def read(k):
            n = i * levels + k
            return base[n], west_v[n], east_v[n], south_v[n], north_v[n]

        return read

    halo0 = react_and_pack(0, True)
    for k in range(levels):
        mix_send[2 * levels + k] = flags[k].astype(jnp.float32)
    per = LANES // NEAR
    for p in range(pl.cdiv(3 * levels, per)):
        to_east = to_west = jnp.zeros((rows, columns), jnp.float32)
        for at in range(min(per, 3 * levels - p * per)):
            value = mix_send[p * per + at]
            here = (lane >= NEAR * at) & (lane < NEAR * at + NEAR)
            turned = pltpu.roll(value, (NEAR * at + NEAR) % LANES, 1)
            to_east = jnp.where(here, turned, to_east)
            turned = pltpu.roll(value, NEAR * at, 1) if at else value
            to_west = jnp.where(here, turned, to_west)
        strip_send[0, p] = to_east
        strip_send[1, p] = to_west
    sent.extend(seas)
    strips = []
    for i, ds in enumerate((1, -1)):
        for dt in (1, -1, 0):
            strips.append(
                remote(
                    strip_send.at[i],
                    strip_recv.at[i, 1 - dt],
                    strip_ssem.at[i, 1 - dt],
                    strip_rsem.at[i, 1 - dt],
                    sect_at(ds),
                    tile_at(dt),
                )
            )
    sent.extend(strips + halo0)

    def reach(n, when):
        _, s, dt, _ = peers[n]

        @pl.when(later[n] & when)
        def _():
            @pl.when(direct[n])
            def _():
                pl.semaphore_wait(known_sem.at[1 + dt, s], 1)

            begin(n)

    def edges(dt):
        if dt:
            halo0[0 if dt == 1 else 2].start()
        else:
            halo0[1].start()
            halo0[3].start()
        for i in range(2):
            strips[3 * i + (1, -1, 0).index(dt)].start()

    ready = {}
    for dt in (1, -1, 0):
        ready[dt] = True
        for ds in (0, 1, -1):
            if ds or dt:
                ready[dt] = (place(sect_at(ds), tile_at(dt)) < mine) & ready[dt]

        @pl.when(ready[dt])
        def _():
            edges(dt)

    for n in sorted(range(len(peers)), key=lambda n: (near.index(peers[n][0]), n)):
        reach(n, me_t != 0 if peers[n][2] == -1 else True)
    for dt in (0, 1):

        @pl.when(jnp.logical_not(ready[dt]))
        def _():
            edges(dt)

    for n, peer in enumerate(peers):
        if peer[2] == -1:
            reach(n, me_t == 0)

    @pl.when(jnp.logical_not(ready[-1]))
    def _():
        edges(-1)

    rest = remote(mix_send, mix_recv, mix_ssem.at[0], mix_rsem.at[0], me_s, 0)

    @pl.when(me_t == tiles - 1)
    def _():
        rest.start()


    for copy in seas:
        copy.wait_recv()

    def blk_wait(j, s):
        blk_copy(j, s, blk_ssem.at[0, 0], me_s, me_t, me_s).wait_recv()

    for j in (0, 2):
        blk_wait(j, me_s)
    in_edge = (lane < EDGE) | (lane >= LANES - EDGE)

    def wet_band(j):
        turned = pltpu.roll(blk_recv[j, me_s, 3], LANES - 6 * EDGE, 1)
        return jnp.concatenate([sea_recv[j], jnp.where(in_edge, turned, 0.0)], axis=1)

    for j in range(bands):
        wet_all[j * rows : (j + 1) * rows] = wet_band(j)
    centre = slice(rows, 2 * rows)

    def first_levels(group, slots, wet, target):
        for l in [group * FIRST * depth + ld for ld in range(FIRST * depth)]:
            s, ld = l // depth, lax.rem(l, depth)
            full = []
            packed = [blk_recv[j, s, 4 * ld + 3] for j in slots]
            for f in range(3):
                parts = []
                for j, pack in zip(slots, packed):
                    turned = pltpu.roll(pack, LANES - 2 * EDGE * f, 1) if f else pack
                    parts.append(jnp.concatenate([blk_recv[j, s, 4 * ld + f], turned], axis=1))
                full.append(jnp.concatenate(parts, axis=0))
            z, m, h, zm, mm = ocean_steps(*full, wet, None, (centre, slice(None)))
            for f, value in enumerate((z, m, h)):
                state[target, 3 * l + f] = value[:, 0:columns]
                state_edge[target, 3 * l + f] = value[:, columns:]
            for i, value in enumerate((zm, mm)):
                means[target, l, i] = value

    def first_interval(group, carry):
        for s in [group * FIRST + at for at in range(FIRST)]:

            @pl.when(s != me_s)
            def _():
                for j in range(bands):
                    blk_wait(j, s)

        first_levels(group, (0, 1, 2), wet_all[...], 1)
        return carry

    def beyond_interval(group, carry):
        first_levels(group, (far, 0, 1), jnp.concatenate([wet_band(far), wet_all[0 : 2 * rows]], axis=0), 0)
        return carry

    lax.fori_loop(0, sects // FIRST, first_interval, 0)

    pair = LANES // (2 * NEAR)

    def pack_edges(buffer, slot, values):
        start = buffer.shape[1] - pl.cdiv(len(values), pair)
        for p in range(pl.cdiv(len(values), pair)):
            tile = values[p * pair]
            for i, value in enumerate(values[p * pair + 1 : (p + 1) * pair], 1):
                here = (lane >= 2 * NEAR * i - NEAR) & (lane < 2 * NEAR * i + NEAR)
                tile = jnp.where(here, pltpu.roll(value, 2 * NEAR * i, 1), tile)
            buffer[slot, start + p] = tile

    def with_edges(buffer, slot, q, count):
        start = buffer.shape[1] - pl.cdiv(count, pair)
        p, at = divmod(q, pair)
        edge = buffer[slot, start + p]
        if at:
            edge = pltpu.roll(edge, LANES - 2 * NEAR * at, 1)
        return jnp.concatenate([buffer[slot, q], edge], axis=1)

    pack_edges(state, 1, [state_edge[1, q] for q in range(3 * levels)])

    def neighbours(buffer, send, recv):
        return [
            remote(buffer.at[1], buffer.at[0], send.at[0], recv.at[0], me_s, tile_at(1)),
            remote(buffer.at[1], buffer.at[2], send.at[1], recv.at[1], me_s, tile_at(-1)),
        ]

    states = neighbours(state, state_ssem, state_rsem)
    forces = neighbours(force, force_ssem, force_rsem)

    def hand_on(copies):
        @pl.when(me_t != 0)
        def _():
            copies[1].start()

        @pl.when(me_t != tiles - 1)
        def _():
            copies[0].start()

    hand_on(states)
    half_wet = tracer_step * wet_cols

    def first_tracers():
        upwind = [flags[k] == 1 for k in range(levels)]
        speeds = [tuple(means[1, k, i, :, 0:columns] for i in range(2)) for k in range(levels)]
        terms = column_terms(speeds, upwind, half_wet, kappa_in)
        shift_cells(0)
        for i in range(tracers):
            for k, value in enumerate(solve_column(terms, tracer_cells(i))):
                conc[i, k] = value
        for copy in react_and_pack(1, False):
            copy.start()

    halo1 = halo_copies(1, cells)
    sent.extend(halo1)
    for copy in halo0:
        copy.wait_recv()

    @pl.when(me_t == 0)
    def _():
        first_tracers()

    for copy in strips:
        copy.wait_recv()

    def halo_tile(q, j):
        p, at = divmod(q, per)
        west_part = pltpu.roll(strip_recv[0, j, p], LANES - NEAR - NEAR * at, 1)
        east_part = strip_recv[1, j, p]
        if at:
            east_part = pltpu.roll(east_part, LANES - NEAR * at, 1)
        return jnp.where(low_half, east_part, west_part)

    def wide_tile(q, j):
        return jnp.concatenate([mix_send[q] if j == 1 else mix_recv[q], halo_tile(q, j)], axis=1)

    wide = columns + LANES

    def heat_band(j):
        speeds = [(means[j, k, 0], means[j, k, 1]) for k in range(levels)]
        upwind = [wide_tile(2 * levels + k, j) > 0.5 for k in range(levels)]
        terms = column_terms(speeds, upwind, tracer_step * wet_all[j * rows : (j + 1) * rows], kappa_in)
        first = lax.broadcasted_iota(jnp.int32, (rows, wide), 0) == 0
        last = lax.broadcasted_iota(jnp.int32, (rows, wide), 0) == rows - 1

        def row_beside(k, i, side):
            at = slice(rows - 1, rows) if i == 0 else slice(0, 1)
            if i == 1:
                return wide_tile(k, 1)[at]
            return jnp.concatenate([rows_recv[0, side, pl.ds(cells + k, 1)], halo_tile(k, i)[at]], axis=1)

        def heat_cells(k):
            d = wide_tile(k, j)
            south, north = pltpu.roll(d, 1, 0), pltpu.roll(d, rows - 1, 0)
            if j == 1:
                south = jnp.where(first, jnp.broadcast_to(row_beside(k, 0, 0), d.shape), south)
            north = jnp.where(last, jnp.broadcast_to(row_beside(k, j + 1, 1), d.shape), north)
            return wide_tile(levels + k, j), pltpu.roll(d, 1, 1), pltpu.roll(d, wide - 1, 1), south, north

        edges = []
        for k, value in enumerate(solve_column(terms, heat_cells)):
            value = (time_step * heat_coupling) * (light_in[k] * value)
            force[j, k] = value[:, 0:columns]
            edges.append(value[:, columns:])
        pack_edges(force, j, edges)

    heat_band(1)
    hand_on(forces)

    @pl.when(me_t == 0)
    def _():
        states[1].start()
        forces[1].start()

    @pl.when(me_t != 0)
    def _():
        first_tracers()

    @pl.when(me_t == 0)
    def _():
        over[sects].wait_recv()
        for s in range(sects):
            blk_wait(far, s)
        lax.fori_loop(0, sects // FIRST, beyond_interval, 0)
        pack_edges(state, 0, [state_edge[0, q] for q in range(3 * levels)])
        rest.wait_recv()
        heat_band(0)

    states[1].wait_recv()
    forces[1].wait_recv()

    @pl.when(me_t != 0)
    def _():
        states[0].wait_recv()
        forces[0].wait_recv()

    def out_copy(l):
        owner, ld = l // depth, l % depth
        return remote(
            out_send.at[l], out_recv.at[me_s, ld], out_ssem.at[l], out_rsem.at[me_s, ld], owner, me_t
        )

    def second_interval(group):
        for l in [group * SECOND + at for at in range(SECOND)]:
            whole = [
                jnp.concatenate([with_edges(state, j, 3 * l + f, 3 * levels) for j in range(bands)], axis=0)
                for f in range(3)
            ]
            forced = jnp.concatenate([with_edges(force, j, l, levels) for j in range(bands)], axis=0)
            z, m, h, zm, mm = ocean_steps(*whole, wet_all[...], forced, (centre, slice(0, columns)))
            last_means[l, 0] = zm
            last_means[l, 1] = mm
            for f, value in enumerate((z, m, h)):
                out_send[l, f] = value
        for l in [group * SECOND + at for at in range(SECOND)]:

            @pl.when(l // depth != me_s)
            def _():
                out_copy(l).start()

    for group in range(levels // SECOND):
        second_interval(group)
    for ld in range(depth):
        out_recv[me_s, ld] = out_send[me_s * depth + ld]

    upwind = [flags[k] == 1 for k in range(levels)]
    speeds = [(last_means[k, 0], last_means[k, 1]) for k in range(levels)]
    terms = column_terms(speeds, upwind, half_wet, kappa_in)
    for copy in halo1:
        copy.wait_recv()
    shift_cells(1)
    for i in range(tracers):
        for k, value in enumerate(solve_column(terms, tracer_cells(i))):
            conc_out[i, k] = value

    def gather(s, carry):
        @pl.when(s != me_s)
        def _():
            for ld in range(depth):
                remote(
                    out_send.at[0], out_recv.at[s, ld], out_ssem.at[0], out_rsem.at[s, ld], me_s, me_t
                ).wait_recv()

        return carry

    lax.fori_loop(0, sects, gather, 0)
    for s in range(sects):
        for ld in range(depth):
            for f, ref in enumerate((zonal_out, merid_out, height_out)):
                ref[ld, :, lanes_of(s)] = out_recv[s, ld, f]
    for copy in sent + [states[1], forces[1]]:
        copy.wait_send()

    for copy in to_peer:
        copy.wait_send()

    @pl.when(me_t != tiles - 1)
    def _():
        states[0].wait_send()
        forces[0].wait_send()

    @pl.when(me_t == tiles - 1)
    def _():
        rest.wait_send()

    @pl.when(me_t == tiles - 2)
    def _():
        for copy in over:
            copy.wait_send()


    def drain(l, carry):
        @pl.when(l // depth != me_s)
        def _():
            out_copy(l).wait_send()

        return carry

    lax.fori_loop(0, levels, drain, 0)


def put_out(*refs):
    copies = [
        pltpu.make_async_copy(src, dst, refs[8].at[i])
        for i, (src, dst) in enumerate(zip(refs[:4], refs[4:8]))
    ]
    for copy in copies:
        copy.start()
    for copy in copies:
        copy.wait()


def body(sects, tiles, zonal, merid, height, level_kappa, sea, flags, conc, react, absorb, light):
    tracers, levels, rows, columns = conc.shape
    depth, _, wide = zonal.shape
    assert rows >= NEAR and columns == LANES and INTERVALS == 2
    assert tiles > 3 and sects % FIRST == 0 and levels % SECOND == 0 and levels == sects * depth and wide == sects * columns
    cells = tracers * levels
    packs = pl.cdiv(cells, LANES)
    padded = pl.cdiv(cells + levels, 8) * 8
    strips = pl.cdiv(3 * levels, LANES // NEAR)
    pair = LANES // (2 * NEAR)
    f32 = jnp.float32
    dma = pltpu.SemaphoreType.DMA
    any_space = pl.BlockSpec(memory_space=pl.ANY)
    vmem = pl.BlockSpec(memory_space=pltpu.VMEM)
    results = pl.pallas_call(
        functools.partial(kernel, sects, tiles),
        out_shape=[
            pltpu.VMEM(conc.shape, f32),
            pltpu.VMEM(zonal.shape, f32),
            pltpu.VMEM(merid.shape, f32),
            pltpu.VMEM(height.shape, f32),
        ],
        in_specs=[pl.BlockSpec(memory_space=pltpu.HBM)] * 10,
        out_specs=[vmem] * 4,
        scratch_shapes=[
            pltpu.SMEM(level_kappa.shape, f32),
            pltpu.SMEM(react.shape, f32),
            pltpu.SMEM(absorb.shape, f32),
            pltpu.SMEM(light.shape, f32),
            pltpu.VMEM((3, depth, rows, wide), f32),
            pltpu.VMEM((rows, wide), jnp.int32),
            pltpu.VMEM(flags.shape, jnp.int32),
            pltpu.VMEM(conc.shape, f32),
        ]
        + [pltpu.VMEM((cells, rows, columns), f32)] * 6
        + [
            pltpu.VMEM((2, 2, packs, rows, columns), f32),
            pltpu.VMEM((2, 2, packs, rows, columns), f32),
            pltpu.VMEM((2, 2, padded, columns), f32),
            pltpu.VMEM((2, 2, padded, columns), f32),
            pltpu.VMEM((sects, 4 * depth, rows, columns), f32),
            pltpu.VMEM((4, sects, 4 * depth, rows, columns), f32),
            pltpu.VMEM((rows, columns), f32),
            pltpu.VMEM((4, rows, columns), f32),
            pltpu.VMEM((3 * levels, rows, columns), f32),
            pltpu.VMEM((3 * levels, rows, columns), f32),
            pltpu.VMEM((2, strips, rows, columns), f32),
            pltpu.VMEM((2, 3, strips, rows, columns), f32),
            pltpu.VMEM((3 * rows, columns + LANES), f32),
            pltpu.VMEM((3, 3 * levels + pl.cdiv(3 * levels, pair), rows, columns), f32),
            pltpu.VMEM((2, 3 * levels, rows, columns), f32),
            pltpu.VMEM((2, levels, 2, rows, columns + LANES), f32),
            pltpu.VMEM((levels, 2, rows, columns), f32),
            pltpu.VMEM((3, levels + pl.cdiv(levels, pair), rows, columns), f32),
            pltpu.VMEM((levels, 3, rows, columns), f32),
            pltpu.VMEM((sects, depth, 3, rows, columns), f32),
            dma((10,)),
            dma((4, sects)),
            dma((4, sects)),
            dma((4,)),
            dma((4,)),
            dma((1,)),
            dma((1,)),
            dma((2,)),
            dma((2,)),
            dma((2,)),
            dma((2,)),
            dma((2, 3)),
            dma((2, 3)),
            dma((2, 4)),
            dma((2, 4)),
            dma((levels,)),
            dma((sects, depth)),
            pltpu.SemaphoreType.REGULAR((3, sects)),
        ],
        compiler_params=pltpu.CompilerParams(collective_id=0, has_side_effects=True),
        name="coupled",
    )(zonal, merid, height, sea, flags, conc, level_kappa, react, absorb, light)
    return pl.pallas_call(
        put_out,
        out_shape=[jax.ShapeDtypeStruct(r.shape, f32) for r in results],
        in_specs=[vmem] * 4,
        out_specs=[any_space] * 4,
        scratch_shapes=[dma((4,))],
        name="put_out",
    )(*[pltpu.with_memory_space_constraint(r, pltpu.VMEM) for r in results])


def solution(mesh):
    placed = (
        P("sect", "tile", None),
        P("sect", "tile", None),
        P("sect", "tile", None),
        P(),
        P("tile", None),
        P(None, "tile", "sect"),
        P(None, None, "tile", "sect"),
        P(),
        P(),
        P(),
    )
    return jax.shard_map(
        functools.partial(body, mesh.shape["sect"], mesh.shape["tile"]),
        mesh=mesh,
        in_specs=placed,
        out_specs=(
            P(None, None, "tile", "sect"),
            P("sect", "tile", None),
            P("sect", "tile", None),
            P("sect", "tile", None),
        ),
        check_vma=False,
    )
```

```python
import functools

import jax
import jax.numpy as jnp
from jax import lax
from jax.experimental import pallas as pl
from jax.experimental.pallas import tpu as pltpu
from jax.sharding import PartitionSpec as P

STEPS = 4
INTERVALS = 2

time_step = 0.1
gravity = 1.0
coriolis = 0.3
viscosity = 0.05
heat_coupling = 0.05
tracer_step = 0.5
stir_gain = 4.0

LANES = 128
EDGE = 4 * STEPS
NEAR = EDGE // 2
FIRST = 4
SECOND = 3


def ocean_steps(zonal, merid, height, wet, forced, keep):
    tall, wide = zonal.shape

    def east(a):
        return pltpu.roll(a, wide - 1, 1)

    def west(a):
        return pltpu.roll(a, 1, 1)

    def north(a):
        return pltpu.roll(a, tall - 1, 0)

    def south(a):
        return pltpu.roll(a, 1, 0)

    keep_rate = time_step * viscosity
    self_rate = 1.0 / keep_rate - 4.0
    turn_rate = time_step * coriolis / keep_rate
    steep = 0.5 * gravity * time_step / keep_rate
    gain = keep_rate * wet
    rise = steep * height
    if forced is not None:
        forced = steep * forced
    zonal_sum = merid_sum = None
    for step in range(STEPS):
        ze, zw, zn, zs = east(zonal), west(zonal), north(zonal), south(zonal)
        me, mw, mn, ms = east(merid), west(merid), north(merid), south(merid)
        rise = rise - (0.5 * time_step * steep) * ((ze - zw) + (mn - ms))
        zonal_part = ((ze + zw) + (zn + zs)) + (self_rate * zonal + turn_rate * merid)
        merid_part = ((me + mw) + (mn + ms)) + (self_rate * merid - turn_rate * zonal)
        if forced is not None:
            rise = rise + forced
        zonal_new = gain * (zonal_part - (east(rise) - west(rise)))
        merid_new = gain * (merid_part - (north(rise) - south(rise)))
        zonal, merid = zonal_new, merid_new
        zonal_sum = zonal[keep] if step == 0 else zonal_sum + zonal[keep]
        merid_sum = merid[keep] if step == 0 else merid_sum + merid[keep]
    return zonal[keep], merid[keep], (1.0 / steep) * rise[keep], zonal_sum / STEPS, merid_sum / STEPS


def column_terms(speeds, upwind, half_wet, kappa_in):
    levels = len(speeds)
    kappa, stencil = [], []
    for k in range(levels):
        along_x, along_y = speeds[k]
        kappa.append(kappa_in[k] * (1.0 + stir_gain * (along_x * along_x + along_y * along_y)))
        terms = []
        for speed in (along_x, along_y):
            terms.append(half_wet * jnp.where(upwind[k], jnp.maximum(speed, 0.0), 0.5 * speed))
            terms.append(half_wet * jnp.where(upwind[k], jnp.minimum(speed, 0.0), 0.5 * speed))
        stencil.append(terms)
    couple = [tracer_step * 0.5 * (kappa[k] + kappa[k + 1]) for k in range(levels - 1)]
    out, factor = [], None
    for k in range(levels):
        denom = 1.0
        if k > 0:
            denom = denom + couple[k - 1]
        if k < levels - 1:
            denom = denom + couple[k]
        if k > 0:
            denom = denom + couple[k - 1] * factor
        inverse = 1.0 / denom
        px, qx, py, qy = stencil[k]
        out.append(
            dict(
                centre=inverse * (1.0 - ((px - qx) + (py - qy))),
                west=inverse * px,
                east=inverse * qx,
                south=inverse * py,
                north=inverse * qy,
                lower=inverse * couple[k - 1] if k > 0 else None,
                upper=inverse * couple[k] if k < levels - 1 else None,
            )
        )
        factor = -out[k]["upper"] if k < levels - 1 else None
    return out


def solve_column(terms, cells):
    levels = len(terms)
    partial = []
    for k in range(levels):
        t = terms[k]
        base, west, east, south, north = cells(k)
        now = t["centre"] * base + (t["west"] * west - t["east"] * east) + (t["south"] * south - t["north"] * north)
        if k > 0:
            now = now + t["lower"] * partial[k - 1]
        partial.append(now)
    for k in range(levels - 2, -1, -1):
        partial[k] = partial[k] + terms[k]["upper"] * partial[k + 1]
    return partial


def kernel(
    sects,
    tiles,
    zonal_in,
    merid_in,
    height_in,
    sea_in,
    flags_in,
    conc_in,
    kappa_hbm,
    react_hbm,
    absorb_hbm,
    light_hbm,
    conc_out,
    zonal_out,
    merid_out,
    height_out,
    kappa_in,
    react_in,
    absorb_in,
    light_in,
    own,
    sea,
    flags,
    conc,
    react_d,
    base,
    west_v,
    east_v,
    south_v,
    north_v,
    cols_send,
    cols_recv,
    rows_send,
    rows_recv,
    blk_send,
    blk_recv,
    sea_send,
    sea_recv,
    mix_send,
    mix_recv,
    strip_send,
    strip_recv,
    wet_all,
    state,
    state_edge,
    means,
    last_means,
    force,
    out_send,
    out_recv,
    local_sem,
    blk_ssem,
    blk_rsem,
    sea_ssem,
    sea_rsem,
    mix_ssem,
    mix_rsem,
    state_ssem,
    state_rsem,
    force_ssem,
    force_rsem,
    strip_ssem,
    strip_rsem,
    halo_ssem,
    halo_rsem,
    out_ssem,
    out_rsem,
    known_sem,
):
    me_s = lax.axis_index("sect")
    me_t = lax.axis_index("tile")
    tracers, levels, rows, columns = conc_in.shape
    depth = zonal_in.shape[0]
    bands = 3
    far = bands

    def sect_at(offset):
        return lax.rem(me_s + (offset + sects), sects)

    def tile_at(offset):
        return lax.rem(me_t + (offset + tiles), tiles)

    def place(s, t):
        hops = t // 2
        for bit in range((sects - 1).bit_length()):
            hops = hops + lax.rem(s // (1 << bit), 2)
        return ((2 * hops + 1 - lax.rem(t, 2)) * tiles + t) * sects + s

    def across(m):
        s = me_s
        for bit in range((sects - 1).bit_length()):
            if m >> bit & 1:
                s = s + (1 << bit) - 2 * (1 << bit) * lax.rem(me_s // (1 << bit), 2)
        return s

    near = sorted(range(sects), key=lambda m: (m.bit_count(), m))
    peers = [(m, across(m), dt, tile_at(dt)) for dt in (1, 0, -1) for m in near if m or dt]
    bits = [lax.rem(me_s // (1 << bit), 2) for bit in range((sects - 1).bit_length())]
    rows_of = {dt: (2 * (t // 2) + 1 - lax.rem(t, 2), t) for dt, t in ((dt, tile_at(dt)) for dt in (1, 0, -1))}
    hops_of = {m: sum((1 - b if m >> i & 1 else b) for i, b in enumerate(bits)) for m in near}
    spots = {
        (m, dt): ((2 * hops_of[m] + rows_of[dt][0]) * tiles + rows_of[dt][1]) * sects + across(m)
        for m in near
        for dt in (1, 0, -1)
    }
    mine = spots[0, 0]
    later, sooner, direct, answer = [], [], [], []
    for m, s, dt, t in peers:
        spot = spots[m, dt]
        later.append(spot > mine)
        sooner.append(spot < mine)
        if m and dt:
            direct.append(spot > spots[0, dt])
            answer.append((spot < mine) & (mine > spots[m, 0]))
        else:
            direct.append(True)
            answer.append(spot < mine)

    def remote(src, dst, send, recv, to_s, to_t):
        return pltpu.make_async_remote_copy(
            src_ref=src,
            dst_ref=dst,
            send_sem=send,
            recv_sem=recv,
            device_id=(to_s, to_t),
            device_id_type=pl.DeviceIdType.MESH,
        )

    fields_in = (zonal_in, merid_in, height_in)
    ocean_local = [pltpu.make_async_copy(field, own.at[f], local_sem.at[f]) for f, field in enumerate(fields_in)]
    ocean_local.append(pltpu.make_async_copy(sea_in, sea, local_sem.at[3]))
    tracer_local = [
        pltpu.make_async_copy(src, dst, local_sem.at[4 + i])
        for i, (src, dst) in enumerate(
            (
                (conc_in, conc),
                (flags_in, flags),
                (react_hbm, react_in),
                (absorb_hbm, absorb_in),
                (kappa_hbm, kappa_in),
                (light_hbm, light_in),
            )
        )
    ]
    barrier = pltpu.get_barrier_semaphore()
    @pl.when(me_t == 0)
    def _():
        for s in [across(m) for m in near[::-1]]:
            pl.semaphore_signal(barrier, inc=1, device_id=(s, tiles - 2), device_id_type=pl.DeviceIdType.MESH)

    heard = 0
    for n, (_, s, _, t) in reversed(list(enumerate(peers))):
        heard = heard + jnp.where(later[n], 0, 1)

        @pl.when(later[n])
        def _():
            pl.semaphore_signal(barrier, inc=1, device_id=(s, t), device_id_type=pl.DeviceIdType.MESH)

    for copy in ocean_local + tracer_local:
        copy.start()
    heard = heard + jnp.where(me_t == tiles - 2, sects, 0)

    @pl.when(heard > 0)
    def _():
        pl.semaphore_wait(barrier, heard)

    for n, (_, s, dt, t) in enumerate(peers):

        @pl.when(answer[n])
        def _():
            pl.semaphore_signal(
                known_sem.at[1 - dt, me_s], inc=1, device_id=(s, t), device_id_type=pl.DeviceIdType.MESH
            )

    lane = lax.broadcasted_iota(jnp.int32, (rows, columns), 1)
    row = lax.broadcasted_iota(jnp.int32, (rows, columns), 0)
    low_half = lane < LANES // 2

    for copy in ocean_local:
        copy.wait()

    def lanes_of(s):
        return slice((s % sects) * columns, (s % sects + 1) * columns)

    sea_f = [sea[:, lanes_of(s)].astype(jnp.float32) for s in range(sects)]
    for d in range(sects):
        for ld in range(depth):
            packed = None
            for f in range(4):
                if f < 3:
                    blk_send[d, 4 * ld + f] = own[f, ld, :, lanes_of(d)]
                    after, before = own[f, ld, :, lanes_of(d + 1)], own[f, ld, :, lanes_of(d - 1)]
                else:
                    after, before = sea_f[(d + 1) % sects], sea_f[(d - 1) % sects]
                edge = jnp.where(low_half, after, before)
                if f == 0:
                    packed = edge
                else:
                    inside = (lane >= 2 * EDGE * f - EDGE) & (lane < 2 * EDGE * f + EDGE)
                    packed = jnp.where(inside, pltpu.roll(edge, 2 * EDGE * f, 1), packed)
            blk_send[d, 4 * ld + 3] = packed
    own_columns = pl.ds(pl.multiple_of(me_s * columns, LANES), columns)
    wet_cols = sea[:, own_columns].astype(jnp.float32)
    is_wet = wet_cols == 1.0
    sea_send[...] = wet_cols

    def blk_copy(j, s_slot, send, to_s, to_t, src):
        return remote(blk_send.at[src], blk_recv.at[j, s_slot], send, blk_rsem.at[j, s_slot], to_s, to_t)

    sent = []
    to_peer = [
        blk_copy(1 - dt, me_s, blk_ssem.at[1 + dt, s], s, t, s) for _, s, dt, t in peers
    ]
    seas = [
        remote(sea_send, sea_recv.at[1 - dt], sea_ssem.at[1 + dt], sea_rsem.at[1 - dt], me_s, tile_at(dt))
        for dt in (1, -1)
    ]
    over = [blk_copy(far, me_s, blk_ssem.at[far, across(m)], across(m), 0, across(m)) for m in near[::-1]]
    over.append(remote(sea_send, sea_recv.at[far], sea_ssem.at[far], sea_rsem.at[far], me_s, 0))

    def begin(n):
        m, _, dt, _ = peers[n]
        if not m:
            seas[0 if dt == 1 else 1].start()
        to_peer[n].start()

    for n in sorted(range(len(peers)), key=lambda n: (-peers[n][2] % bands, -n)):

        @pl.when(sooner[n])
        def _():
            begin(n)

    @pl.when(me_t == tiles - 2)
    def _():
        for copy in over[sects:] + over[:sects]:
            copy.start()

    blk_recv[1, me_s] = blk_send[me_s]
    sea_recv[1] = sea_send[...]
    for copy in tracer_local:
        copy.wait()

    cells = tracers * levels

    def react_and_pack(turn, heated):
        names = tracers + (1 if heated else 0)
        to_east = [jnp.zeros((rows, columns), jnp.float32) for _ in range(pl.cdiv(cells, LANES))]
        to_west = list(to_east)
        for k in range(levels):
            old = [conc[i, k] for i in range(tracers)]
            heat_d = None
            for i in range(names):
                n = i * levels + k
                if i < tracers:
                    growth = react_in[i, 0] * old[0]
                    for j in range(1, tracers):
                        growth = growth + react_in[i, j] * old[j]
                    new = old[i] + tracer_step * growth
                    kept = jnp.where(is_wet, new, old[i])
                    if heated:
                        a = absorb_in[i]
                        heat_d = a * new if i == 0 else heat_d + a * new
                        heat_b = a * kept if i == 0 else heat_b + a * kept
                else:
                    mix_send[k] = heat_d
                    mix_send[levels + k] = heat_b
                    rows_send[turn, 0, pl.ds(n, 1)] = heat_d[rows - 1 : rows]
                    rows_send[turn, 1, pl.ds(n, 1)] = heat_d[0:1]
                    continue
                react_d[n] = new
                base[n] = kept
                rows_send[turn, 0, pl.ds(n, 1)] = new[rows - 1 : rows]
                rows_send[turn, 1, pl.ds(n, 1)] = new[0:1]
                p, at = divmod(n, LANES)
                here = lane == at
                turned = pltpu.roll(new, (at + 1) % columns, 1)
                to_east[p] = jnp.where(here, turned, to_east[p])
                turned = pltpu.roll(new, at, 1) if at else new
                to_west[p] = jnp.where(here, turned, to_west[p])
        for p in range(len(to_east)):
            cols_send[turn, 0, p] = to_east[p]
            cols_send[turn, 1, p] = to_west[p]
        return halo_copies(turn, names * levels)

    def halo_copies(turn, count):
        tall = pl.cdiv(count, 8) * 8
        copies = []
        for i, d in enumerate((1, -1)):
            copies.append(
                remote(
                    rows_send.at[turn, i, pl.ds(0, tall)],
                    rows_recv.at[turn, i, pl.ds(0, tall)],
                    halo_ssem.at[turn, i],
                    halo_rsem.at[turn, i],
                    me_s,
                    tile_at(d),
                )
            )
            copies.append(
                remote(
                    cols_send.at[turn, i],
                    cols_recv.at[turn, i],
                    halo_ssem.at[turn, 2 + i],
                    halo_rsem.at[turn, 2 + i],
                    sect_at(d),
                    me_t,
                )
            )
        return copies

    def shift_cells(turn):
        from_west = [cols_recv[turn, 0, p] for p in range(pl.cdiv(cells, LANES))]
        from_east = [cols_recv[turn, 1, p] for p in range(pl.cdiv(cells, LANES))]
        for n in range(cells):
            p, at = divmod(n, LANES)
            new = react_d[n]
            edge = pltpu.roll(from_west[p], columns - at, 1) if at else from_west[p]
            west_v[n] = jnp.where(lane == 0, edge, pltpu.roll(new, 1, 1))
            edge = pltpu.roll(from_east[p], columns - 1 - at, 1) if at < columns - 1 else from_east[p]
            east_v[n] = jnp.where(lane == columns - 1, edge, pltpu.roll(new, columns - 1, 1))
            edge = jnp.broadcast_to(rows_recv[turn, 0, pl.ds(n, 1)], (rows, columns))
            south_v[n] = jnp.where(row == 0, edge, pltpu.roll(new, 1, 0))
            edge = jnp.broadcast_to(rows_recv[turn, 1, pl.ds(n, 1)], (rows, columns))
            north_v[n] = jnp.where(row == rows - 1, edge, pltpu.roll(new, rows - 1, 0))

    def tracer_cells(i):
        def read(k):
            n = i * levels + k
            return base[n], west_v[n], east_v[n], south_v[n], north_v[n]

        return read

    halo0 = react_and_pack(0, True)
    for k in range(levels):
        mix_send[2 * levels + k] = flags[k].astype(jnp.float32)
    per = LANES // NEAR
    for p in range(pl.cdiv(3 * levels, per)):
        to_east = to_west = jnp.zeros((rows, columns), jnp.float32)
        for at in range(min(per, 3 * levels - p * per)):
            value = mix_send[p * per + at]
            here = (lane >= NEAR * at) & (lane < NEAR * at + NEAR)
            turned = pltpu.roll(value, (NEAR * at + NEAR) % LANES, 1)
            to_east = jnp.where(here, turned, to_east)
            turned = pltpu.roll(value, NEAR * at, 1) if at else value
            to_west = jnp.where(here, turned, to_west)
        strip_send[0, p] = to_east
        strip_send[1, p] = to_west
    sent.extend(seas)
    strips = []
    for i, ds in enumerate((1, -1)):
        for dt in (1, -1, 0):
            strips.append(
                remote(
                    strip_send.at[i],
                    strip_recv.at[i, 1 - dt],
                    strip_ssem.at[i, 1 - dt],
                    strip_rsem.at[i, 1 - dt],
                    sect_at(ds),
                    tile_at(dt),
                )
            )
    sent.extend(strips + halo0)

    def reach(n, when):
        _, s, dt, _ = peers[n]

        @pl.when(later[n] & when)
        def _():
            @pl.when(direct[n])
            def _():
                pl.semaphore_wait(known_sem.at[1 + dt, s], 1)

            begin(n)

    def edges(dt):
        if dt:
            halo0[0 if dt == 1 else 2].start()
        else:
            halo0[1].start()
            halo0[3].start()
        for i in range(2):
            strips[3 * i + (1, -1, 0).index(dt)].start()

    ready = {}
    for dt in (1, -1, 0):
        ready[dt] = True
        for ds in (0, 1, -1):
            if ds or dt:
                ready[dt] = (place(sect_at(ds), tile_at(dt)) < mine) & ready[dt]

        @pl.when(ready[dt])
        def _():
            edges(dt)

    for n in sorted(range(len(peers)), key=lambda n: (near.index(peers[n][0]), n)):
        reach(n, me_t != 0 if peers[n][2] == -1 else True)
    for dt in (0, 1):

        @pl.when(jnp.logical_not(ready[dt]))
        def _():
            edges(dt)

    for n, peer in enumerate(peers):
        if peer[2] == -1:
            reach(n, me_t == 0)

    @pl.when(jnp.logical_not(ready[-1]))
    def _():
        edges(-1)

    rest = remote(mix_send, mix_recv, mix_ssem.at[0], mix_rsem.at[0], me_s, 0)

    @pl.when(me_t == tiles - 1)
    def _():
        rest.start()


    for copy in seas:
        copy.wait_recv()

    def blk_wait(j, s):
        blk_copy(j, s, blk_ssem.at[0, 0], me_s, me_t, me_s).wait_recv()

    for j in (0, 2):
        blk_wait(j, me_s)
    in_edge = (lane < EDGE) | (lane >= LANES - EDGE)

    def wet_band(j):
        turned = pltpu.roll(blk_recv[j, me_s, 3], LANES - 6 * EDGE, 1)
        return jnp.concatenate([sea_recv[j], jnp.where(in_edge, turned, 0.0)], axis=1)

    for j in range(bands):
        wet_all[j * rows : (j + 1) * rows] = wet_band(j)
    centre = slice(rows, 2 * rows)

    def first_levels(group, slots, wet, target):
        for l in [group * FIRST * depth + ld for ld in range(FIRST * depth)]:
            s, ld = l // depth, lax.rem(l, depth)
            full = []
            packed = [blk_recv[j, s, 4 * ld + 3] for j in slots]
            for f in range(3):
                parts = []
                for j, pack in zip(slots, packed):
                    turned = pltpu.roll(pack, LANES - 2 * EDGE * f, 1) if f else pack
                    parts.append(jnp.concatenate([blk_recv[j, s, 4 * ld + f], turned], axis=1))
                full.append(jnp.concatenate(parts, axis=0))
            z, m, h, zm, mm = ocean_steps(*full, wet, None, (centre, slice(None)))
            for f, value in enumerate((z, m, h)):
                state[target, 3 * l + f] = value[:, 0:columns]
                state_edge[target, 3 * l + f] = value[:, columns:]
            for i, value in enumerate((zm, mm)):
                means[target, l, i] = value

    def first_interval(group, carry):
        for s in [group * FIRST + at for at in range(FIRST)]:

            @pl.when(s != me_s)
            def _():
                for j in range(bands):
                    blk_wait(j, s)

        first_levels(group, (0, 1, 2), wet_all[...], 1)
        return carry

    def beyond_interval(group, carry):
        first_levels(group, (far, 0, 1), jnp.concatenate([wet_band(far), wet_all[0 : 2 * rows]], axis=0), 0)
        return carry

    lax.fori_loop(0, sects // FIRST, first_interval, 0)

    pair = LANES // (2 * NEAR)

    def pack_edges(buffer, slot, values):
        start = buffer.shape[1] - pl.cdiv(len(values), pair)
        for p in range(pl.cdiv(len(values), pair)):
            tile = values[p * pair]
            for i, value in enumerate(values[p * pair + 1 : (p + 1) * pair], 1):
                here = (lane >= 2 * NEAR * i - NEAR) & (lane < 2 * NEAR * i + NEAR)
                tile = jnp.where(here, pltpu.roll(value, 2 * NEAR * i, 1), tile)
            buffer[slot, start + p] = tile

    def with_edges(buffer, slot, q, count):
        start = buffer.shape[1] - pl.cdiv(count, pair)
        p, at = divmod(q, pair)
        edge = buffer[slot, start + p]
        if at:
            edge = pltpu.roll(edge, LANES - 2 * NEAR * at, 1)
        return jnp.concatenate([buffer[slot, q], edge], axis=1)

    pack_edges(state, 1, [state_edge[1, q] for q in range(3 * levels)])

    def neighbours(buffer, send, recv):
        return [
            remote(buffer.at[1], buffer.at[0], send.at[0], recv.at[0], me_s, tile_at(1)),
            remote(buffer.at[1], buffer.at[2], send.at[1], recv.at[1], me_s, tile_at(-1)),
        ]

    states = neighbours(state, state_ssem, state_rsem)
    forces = neighbours(force, force_ssem, force_rsem)

    def hand_on(copies):
        @pl.when(me_t != 0)
        def _():
            copies[1].start()

        @pl.when(me_t != tiles - 1)
        def _():
            copies[0].start()

    hand_on(states)
    half_wet = tracer_step * wet_cols

    def first_tracers():
        upwind = [flags[k] == 1 for k in range(levels)]
        speeds = [tuple(means[1, k, i, :, 0:columns] for i in range(2)) for k in range(levels)]
        terms = column_terms(speeds, upwind, half_wet, kappa_in)
        shift_cells(0)
        for i in range(tracers):
            for k, value in enumerate(solve_column(terms, tracer_cells(i))):
                conc[i, k] = value
        for copy in react_and_pack(1, False):
            copy.start()

    halo1 = halo_copies(1, cells)
    sent.extend(halo1)
    for copy in halo0:
        copy.wait_recv()

    @pl.when(me_t == 0)
    def _():
        first_tracers()

    for copy in strips:
        copy.wait_recv()

    def halo_tile(q, j):
        p, at = divmod(q, per)
        west_part = pltpu.roll(strip_recv[0, j, p], LANES - NEAR - NEAR * at, 1)
        east_part = strip_recv[1, j, p]
        if at:
            east_part = pltpu.roll(east_part, LANES - NEAR * at, 1)
        return jnp.where(low_half, east_part, west_part)

    def wide_tile(q, j):
        return jnp.concatenate([mix_send[q] if j == 1 else mix_recv[q], halo_tile(q, j)], axis=1)

    wide = columns + LANES

    def heat_band(j):
        speeds = [(means[j, k, 0], means[j, k, 1]) for k in range(levels)]
        upwind = [wide_tile(2 * levels + k, j) > 0.5 for k in range(levels)]
        terms = column_terms(speeds, upwind, tracer_step * wet_all[j * rows : (j + 1) * rows], kappa_in)
        first = lax.broadcasted_iota(jnp.int32, (rows, wide), 0) == 0
        last = lax.broadcasted_iota(jnp.int32, (rows, wide), 0) == rows - 1

        def row_beside(k, i, side):
            at = slice(rows - 1, rows) if i == 0 else slice(0, 1)
            if i == 1:
                return wide_tile(k, 1)[at]
            return jnp.concatenate([rows_recv[0, side, pl.ds(cells + k, 1)], halo_tile(k, i)[at]], axis=1)

        def heat_cells(k):
            d = wide_tile(k, j)
            south, north = pltpu.roll(d, 1, 0), pltpu.roll(d, rows - 1, 0)
            if j == 1:
                south = jnp.where(first, jnp.broadcast_to(row_beside(k, 0, 0), d.shape), south)
            north = jnp.where(last, jnp.broadcast_to(row_beside(k, j + 1, 1), d.shape), north)
            return wide_tile(levels + k, j), pltpu.roll(d, 1, 1), pltpu.roll(d, wide - 1, 1), south, north

        edges = []
        for k, value in enumerate(solve_column(terms, heat_cells)):
            value = (time_step * heat_coupling) * (light_in[k] * value)
            force[j, k] = value[:, 0:columns]
            edges.append(value[:, columns:])
        pack_edges(force, j, edges)

    heat_band(1)
    hand_on(forces)

    @pl.when(me_t == 0)
    def _():
        states[1].start()
        forces[1].start()

    @pl.when(me_t != 0)
    def _():
        first_tracers()

    @pl.when(me_t == 0)
    def _():
        over[sects].wait_recv()
        for s in range(sects):
            blk_wait(far, s)
        lax.fori_loop(0, sects // FIRST, beyond_interval, 0)
        pack_edges(state, 0, [state_edge[0, q] for q in range(3 * levels)])
        rest.wait_recv()
        heat_band(0)

    states[1].wait_recv()
    forces[1].wait_recv()

    @pl.when(me_t != 0)
    def _():
        states[0].wait_recv()
        forces[0].wait_recv()

    def out_copy(l):
        owner, ld = l // depth, l % depth
        return remote(
            out_send.at[l], out_recv.at[me_s, ld], out_ssem.at[l], out_rsem.at[me_s, ld], owner, me_t
        )

    def second_interval(group):
        for l in group:
            whole = [
                jnp.concatenate([with_edges(state, j, 3 * l + f, 3 * levels) for j in range(bands)], axis=0)
                for f in range(3)
            ]
            forced = jnp.concatenate([with_edges(force, j, l, levels) for j in range(bands)], axis=0)
            z, m, h, zm, mm = ocean_steps(*whole, wet_all[...], forced, (centre, slice(0, columns)))
            last_means[l, 0] = zm
            last_means[l, 1] = mm
            for f, value in enumerate((z, m, h)):
                out_send[l, f] = value
        for l in group:

            @pl.when(l // depth != me_s)
            def _():
                out_copy(l).start()

    second_interval([0])
    for start in range(1, levels, SECOND):
        second_interval(range(start, min(start + SECOND, levels)))
    for ld in range(depth):
        out_recv[me_s, ld] = out_send[me_s * depth + ld]

    upwind = [flags[k] == 1 for k in range(levels)]
    speeds = [(last_means[k, 0], last_means[k, 1]) for k in range(levels)]
    terms = column_terms(speeds, upwind, half_wet, kappa_in)
    for copy in halo1:
        copy.wait_recv()
    shift_cells(1)
    for i in range(tracers):
        for k, value in enumerate(solve_column(terms, tracer_cells(i))):
            conc_out[i, k] = value

    def gather(s, carry):
        @pl.when(s != me_s)
        def _():
            for ld in range(depth):
                remote(
                    out_send.at[0], out_recv.at[s, ld], out_ssem.at[0], out_rsem.at[s, ld], me_s, me_t
                ).wait_recv()

        return carry

    lax.fori_loop(0, sects, gather, 0)
    for s in range(sects):
        for ld in range(depth):
            for f, ref in enumerate((zonal_out, merid_out, height_out)):
                ref[ld, :, lanes_of(s)] = out_recv[s, ld, f]
    for copy in sent + [states[1], forces[1]]:
        copy.wait_send()

    for copy in to_peer:
        copy.wait_send()

    @pl.when(me_t != tiles - 1)
    def _():
        states[0].wait_send()
        forces[0].wait_send()

    @pl.when(me_t == tiles - 1)
    def _():
        rest.wait_send()

    @pl.when(me_t == tiles - 2)
    def _():
        for copy in over:
            copy.wait_send()


    def drain(l, carry):
        @pl.when(l // depth != me_s)
        def _():
            out_copy(l).wait_send()

        return carry

    lax.fori_loop(0, levels, drain, 0)


def put_out(*refs):
    copies = [
        pltpu.make_async_copy(src, dst, refs[8].at[i])
        for i, (src, dst) in enumerate(zip(refs[:4], refs[4:8]))
    ]
    for copy in copies:
        copy.start()
    for copy in copies:
        copy.wait()


def body(sects, tiles, zonal, merid, height, level_kappa, sea, flags, conc, react, absorb, light):
    tracers, levels, rows, columns = conc.shape
    depth, _, wide = zonal.shape
    assert rows >= NEAR and columns == LANES and INTERVALS == 2
    assert tiles > 3 and sects % FIRST == 0 and levels == sects * depth and wide == sects * columns
    cells = tracers * levels
    packs = pl.cdiv(cells, LANES)
    padded = pl.cdiv(cells + levels, 8) * 8
    strips = pl.cdiv(3 * levels, LANES // NEAR)
    pair = LANES // (2 * NEAR)
    f32 = jnp.float32
    dma = pltpu.SemaphoreType.DMA
    any_space = pl.BlockSpec(memory_space=pl.ANY)
    vmem = pl.BlockSpec(memory_space=pltpu.VMEM)
    results = pl.pallas_call(
        functools.partial(kernel, sects, tiles),
        out_shape=[
            pltpu.VMEM(conc.shape, f32),
            pltpu.VMEM(zonal.shape, f32),
            pltpu.VMEM(merid.shape, f32),
            pltpu.VMEM(height.shape, f32),
        ],
        in_specs=[pl.BlockSpec(memory_space=pltpu.HBM)] * 10,
        out_specs=[vmem] * 4,
        scratch_shapes=[
            pltpu.SMEM(level_kappa.shape, f32),
            pltpu.SMEM(react.shape, f32),
            pltpu.SMEM(absorb.shape, f32),
            pltpu.SMEM(light.shape, f32),
            pltpu.VMEM((3, depth, rows, wide), f32),
            pltpu.VMEM((rows, wide), jnp.int32),
            pltpu.VMEM(flags.shape, jnp.int32),
            pltpu.VMEM(conc.shape, f32),
        ]
        + [pltpu.VMEM((cells, rows, columns), f32)] * 6
        + [
            pltpu.VMEM((2, 2, packs, rows, columns), f32),
            pltpu.VMEM((2, 2, packs, rows, columns), f32),
            pltpu.VMEM((2, 2, padded, columns), f32),
            pltpu.VMEM((2, 2, padded, columns), f32),
            pltpu.VMEM((sects, 4 * depth, rows, columns), f32),
            pltpu.VMEM((4, sects, 4 * depth, rows, columns), f32),
            pltpu.VMEM((rows, columns), f32),
            pltpu.VMEM((4, rows, columns), f32),
            pltpu.VMEM((3 * levels, rows, columns), f32),
            pltpu.VMEM((3 * levels, rows, columns), f32),
            pltpu.VMEM((2, strips, rows, columns), f32),
            pltpu.VMEM((2, 3, strips, rows, columns), f32),
            pltpu.VMEM((3 * rows, columns + LANES), f32),
            pltpu.VMEM((3, 3 * levels + pl.cdiv(3 * levels, pair), rows, columns), f32),
            pltpu.VMEM((2, 3 * levels, rows, columns), f32),
            pltpu.VMEM((2, levels, 2, rows, columns + LANES), f32),
            pltpu.VMEM((levels, 2, rows, columns), f32),
            pltpu.VMEM((3, levels + pl.cdiv(levels, pair), rows, columns), f32),
            pltpu.VMEM((levels, 3, rows, columns), f32),
            pltpu.VMEM((sects, depth, 3, rows, columns), f32),
            dma((10,)),
            dma((4, sects)),
            dma((4, sects)),
            dma((4,)),
            dma((4,)),
            dma((1,)),
            dma((1,)),
            dma((2,)),
            dma((2,)),
            dma((2,)),
            dma((2,)),
            dma((2, 3)),
            dma((2, 3)),
            dma((2, 4)),
            dma((2, 4)),
            dma((levels,)),
            dma((sects, depth)),
            pltpu.SemaphoreType.REGULAR((3, sects)),
        ],
        compiler_params=pltpu.CompilerParams(collective_id=0, has_side_effects=True),
        name="coupled",
    )(zonal, merid, height, sea, flags, conc, level_kappa, react, absorb, light)
    return pl.pallas_call(
        put_out,
        out_shape=[jax.ShapeDtypeStruct(r.shape, f32) for r in results],
        in_specs=[vmem] * 4,
        out_specs=[any_space] * 4,
        scratch_shapes=[dma((4,))],
        name="put_out",
    )(*[pltpu.with_memory_space_constraint(r, pltpu.VMEM) for r in results])


def solution(mesh):
    placed = (
        P("sect", "tile", None),
        P("sect", "tile", None),
        P("sect", "tile", None),
        P(),
        P("tile", None),
        P(None, "tile", "sect"),
        P(None, None, "tile", "sect"),
        P(),
        P(),
        P(),
    )
    return jax.shard_map(
        functools.partial(body, mesh.shape["sect"], mesh.shape["tile"]),
        mesh=mesh,
        in_specs=placed,
        out_specs=(
            P(None, None, "tile", "sect"),
            P("sect", "tile", None),
            P("sect", "tile", None),
            P("sect", "tile", None),
        ),
        check_vma=False,
    )
```
